256 devices in a mesh: gx: 16 (over y_lo, x, core), gy: 16 (over y_hi, z).
Axes of the slice: x: 4, y: 4 (y_hi: 2, y_lo: 2; y = y_hi * 2 + y_lo), z: 8, core: 2. Of those that a mesh axis runs over, the one named last changes fastest.
Arguments:
- tensor: bfloat16 [8, 8192, 8192], P(None, 'gx', 'gy'), may hold values from -6 to 6
- y_factor: bfloat16 [8192, 64], P('gy'), may hold values from -0.0625 to 0.0625
- x_factor: bfloat16 [64, 8192], P(None, 'gx'), may hold values from -0.0625 to 0.0625
Outputs:
- new_basis: float32 [64, 8192], P(None, ('gx', 'gy'))
The draws below stay inside these ranges and needn't reach their ends.
All inputs are finite; a program needn't handle non-finite values.
Results may differ from the reference program's by a relative error of at most 0.0003.
Values sent between devices are 32-bit elements; how exact they have to be, the bound alone decides.
No kernel may reach another device: no remote copies, remote signals or barrier semaphores. Data moves between devices by JAX's collectives and lax.ppermute only.
A program may use at most 64 MiB of HBM per device.

```python
import jax
import jax.numpy as jnp
from jax import lax

BX = 512
Z = 8
R = 64
NX = 8192
NY = 8192


def block_scale(rng, dims, shards, least, largest):
    loudness = 1.0
    for axis_at, blocks in shards:
        steps = jax.random.uniform(jax.random.fold_in(jax.random.fold_in(rng, 6), axis_at), (blocks,), jnp.float32, least / len(shards), largest / len(shards))
        loudness = loudness * jnp.repeat(jnp.exp(steps), dims[axis_at] // blocks).reshape((-1,) + (1,) * (len(dims) - 1 - axis_at))
    return loudness


def centred(stream_key, shape, spread, bound, shards=(), kind=jnp.bfloat16):
    level = block_scale(stream_key, shape, shards, -0.22, 0.18) if shards else 1.0
    entries = jax.random.normal(stream_key, shape, jnp.float32) * spread * level
    return jnp.minimum(jnp.maximum(entries, -bound), bound).astype(kind)


def setup_inputs(seed: int = 0) -> dict:
    keys = jax.random.split(jax.random.key(seed), 4)
    tensor = centred(keys[0], (Z, NX, NY), 1.0, 6.0, ((1, 16), (2, 16)))
    y_factor = centred(keys[1], (NY, R), NY ** -0.5, 0.0625, ((0, 16),))
    x_factor = centred(keys[2], (R, NX), NX ** -0.5, 0.0625, ((1, 16),))
    return {"tensor": tensor, "y_factor": y_factor, "x_factor": x_factor}


def reference(tensor, y_factor, x_factor):

    def project_plane(plane):
        return jnp.dot(plane.astype(jnp.float32), y_factor.astype(jnp.float32), preferred_element_type=jnp.float32)
    planes = lax.map(project_plane, tensor)
    proj_rows = jnp.transpose(planes, (0, 2, 1)).reshape(Z * R, NX)
    factor_wide = x_factor.astype(jnp.float32)
    proj_trans = proj_rows.T

    def column_block(index):
        block = lax.dynamic_slice_in_dim(proj_rows, index * BX, BX, 1)
        gram_cols = jnp.dot(proj_trans, block, precision=lax.Precision.HIGHEST)
        return jnp.dot(factor_wide, gram_cols, precision=lax.Precision.HIGHEST)
    blocks = lax.map(column_block, jnp.arange(NX // BX, dtype=jnp.int32))
    update = jnp.transpose(blocks, (1, 0, 2)).reshape(R, NX)
    cross_gram = jnp.dot(update, update.T, precision=lax.Precision.HIGHEST)
    cholesky_factor = jnp.linalg.cholesky(cross_gram)
    solved = jax.scipy.linalg.solve_triangular(cholesky_factor, update, lower=True)
    return solved * jnp.sqrt(jnp.float32(NX))
```

```python
import jax
import jax.numpy as jnp
from jax import lax
from jax.sharding import Mesh
from jax.sharding import PartitionSpec as P

AXES = ("y_lo", "x", "core", "y_hi", "z")
GX = ("y_lo", "x", "core")
GY = ("y_hi", "z")
PLANE = ("y_hi", "y_lo", "x", "core")
CHIPS = ("y_hi", "y_lo", "x")
HIGHEST = lax.Precision.HIGHEST


def exchanged(tiles, axis):
    return lax.all_to_all(tiles, axis, 0, 0, tiled=True)


def of_everyone(tile, axis):
    return exchanged(jnp.broadcast_to(tile[None], (lax.axis_size(axis), *tile.shape)), axis)


def tiles_of(matrix):
    rows, cols = matrix.shape
    return matrix.reshape(rows // 8, 8, cols // 128, 128).swapaxes(1, 2).reshape(-1, 8, 128)


def from_tiles(tiles, rows, cols):
    return tiles.reshape(rows // 8, cols // 128, 8, 128).swapaxes(1, 2).reshape(rows, cols)


def summed_everywhere(matrix):
    rows, cols = matrix.shape
    n = lax.axis_size(PLANE)
    tiles = tiles_of(matrix).reshape(n, -1, 128)
    own = jnp.sum(exchanged(tiles, PLANE), axis=0)
    own = jnp.sum(of_everyone(own, "z"), axis=0)
    return from_tiles(of_everyone(own, PLANE).reshape(-1, 8, 128), rows, cols)


def small_sum(square):
    half = square.shape[0] // 2
    wide = jnp.concatenate([square[:half], square[half:]], axis=1)
    wide = wide + lax.ppermute(wide, "core", [(0, 1), (1, 0)])
    wide = jnp.sum(of_everyone(wide, CHIPS), axis=0)
    wide = jnp.sum(of_everyone(wide, "z"), axis=0)
    return jnp.concatenate([wide[:, : 2 * half], wide[:, 2 * half :]], axis=0)


def per_device(tensor, y_factor, x_factor):
    width_x = tensor.shape[1]
    rank = x_factor.shape[0]
    factor_wide = x_factor.astype(jnp.float32)
    proj_t = jnp.einsum("zxy,yr->xzr", tensor, y_factor, preferred_element_type=jnp.float32)
    proj_t = proj_t.reshape(width_x, -1)
    folded = summed_everywhere(jnp.dot(factor_wide, proj_t, precision=HIGHEST))
    part = lax.dot_general(proj_t, folded, (((1,), (1,)), ((), ())), precision=HIGHEST)
    n = lax.axis_size(GY)
    own_x = width_x // n
    part = part.reshape(n, 2, own_x // 2, rank)
    part = jnp.concatenate([part[:, 0], part[:, 1]], axis=2)
    packed = jnp.sum(exchanged(part, GY), axis=0)
    update_t = jnp.concatenate([packed[:, :rank], packed[:, rank:]], axis=0)
    local_cross = lax.dot_general(update_t, update_t, (((0,), (0,)), ((), ())), precision=HIGHEST)
    cross_gram = small_sum(local_cross)
    cholesky_factor = jnp.linalg.cholesky(cross_gram)
    solved = jax.scipy.linalg.solve_triangular(cholesky_factor, update_t.T, lower=True)
    total_x = width_x * lax.axis_size(GX)
    return solved * jnp.sqrt(jnp.float32(total_x))


def solution(mesh):
    finer = Mesh(mesh.devices.reshape(2, 4, 2, 2, 8), AXES)
    in_specs = (P(None, GX, GY), P(GY, None), P(None, GX))
    out_specs = P(None, AXES)
    return jax.shard_map(
        per_device, mesh=finer, in_specs=in_specs, out_specs=out_specs, check_vma=False
    )
```

```python
import functools

import jax
import jax.numpy as jnp
from jax import lax
from jax.experimental import pallas as pl
from jax.experimental.pallas import tpu as pltpu
from jax.sharding import Mesh
from jax.sharding import PartitionSpec as P

AXES = ("y_lo", "x", "core", "y_hi", "z")
GX = ("y_lo", "x", "core")
GY = ("y_hi", "z")
PLANE = ("y_hi", "y_lo", "x", "core")
CHIPS = ("y_hi", "y_lo", "x")
HIGHEST = lax.Precision.HIGHEST
ON_CHIP = pl.BlockSpec(memory_space=pltpu.VMEM)


def exchanged(tiles, axis):
    return lax.all_to_all(tiles, axis, 0, 0, tiled=True)


def of_everyone(tile, axis):
    return exchanged(jnp.broadcast_to(tile[None], (lax.axis_size(axis), *tile.shape)), axis)


def tiles_of(matrix):
    rows, cols = matrix.shape
    return matrix.reshape(rows // 8, 8, cols // 128, 128).swapaxes(1, 2).reshape(-1, 8, 128)


def from_tiles(tiles, rows, cols):
    return tiles.reshape(rows // 8, cols // 128, 8, 128).swapaxes(1, 2).reshape(rows, cols)


def summed_everywhere(matrix):
    rows, cols = matrix.shape
    n = lax.axis_size(PLANE)
    tiles = tiles_of(matrix).reshape(n, -1, 128)
    own = jnp.sum(exchanged(tiles, PLANE), axis=0)
    own = jnp.sum(of_everyone(own, "z"), axis=0)
    return from_tiles(of_everyone(own, PLANE).reshape(-1, 8, 128), rows, cols)


def cross_terms(wide):
    wide = wide + lax.ppermute(wide, "core", [(0, 1), (1, 0)])
    wide = jnp.sum(of_everyone(wide, CHIPS), axis=0)
    return of_everyone(wide, "z")


def rounded_parts(matrix):
    high = matrix.astype(jnp.bfloat16)
    rest = matrix - high.astype(jnp.float32)
    middle = rest.astype(jnp.bfloat16)
    low = (rest - middle.astype(jnp.float32)).astype(jnp.bfloat16)
    return high, middle, low


def project_kernel(
    tensor_ref,
    y_ref,
    x_ref,
    proj_ref,
    folded_ref,
    planes,
    y_here,
    x_here,
    proj_here,
    folded_here,
    arrived,
    left,
):
    depth = planes.shape[0]
    rank = y_ref.shape[0]
    y_copy = pltpu.make_async_copy(y_ref, y_here, arrived.at[depth])
    x_copy = pltpu.make_async_copy(x_ref, x_here, arrived.at[depth + 1])
    y_copy.start()

    def plane(z):
        return pltpu.make_async_copy(tensor_ref.at[z], planes.at[z], arrived.at[z])

    def results(pair):
        lanes = pl.ds(2 * rank * pair, 2 * rank)
        return [
            pltpu.make_async_copy(here.at[:, lanes], there.at[:, lanes], left.at[pair, i])
            for i, (here, there) in enumerate(
                ((proj_here, proj_ref), (folded_here, folded_ref))
            )
        ]

    for z in range(depth):
        plane(z).start()
    x_copy.start()
    y_copy.wait()
    y_t = y_here[...]
    none = jnp.zeros_like(y_t)
    sides = (jnp.concatenate([y_t, none], axis=0), jnp.concatenate([none, y_t], axis=0))
    contract = (((1,), (1,)), ((), ()))
    for pair in range(depth // 2):
        total = None
        for side in range(2):
            z = 2 * pair + side
            plane(z).wait()
            term = lax.dot_general(
                planes[z], sides[side], contract, preferred_element_type=jnp.float32
            )
            total = term if total is None else total + term
        lanes = pl.ds(2 * rank * pair, 2 * rank)
        proj_here[:, lanes] = total
        proj_copy, folded_copy = results(pair)
        proj_copy.start()
        if pair == 0:
            x_copy.wait()
        folded = None
        for part in rounded_parts(total):
            term = jnp.dot(x_here[...], part, preferred_element_type=jnp.float32)
            folded = term if folded is None else folded + term
        folded_here[:, lanes] = folded
        folded_copy.start()
    for pair in range(depth // 2):
        for copy in results(pair):
            copy.wait()


def projected(tensor, y_factor, x_factor):
    depth, width_x, width_y = tensor.shape
    rank = y_factor.shape[1]
    return pl.pallas_call(
        project_kernel,
        out_shape=[
            jax.ShapeDtypeStruct((width_x, depth * rank), jnp.float32),
            jax.ShapeDtypeStruct((rank, depth * rank), jnp.float32),
        ],
        in_specs=[pl.BlockSpec(memory_space=pltpu.HBM)] * 3,
        out_specs=[pl.BlockSpec(memory_space=pltpu.HBM)] * 2,
        scratch_shapes=[
            pltpu.VMEM(tensor.shape, tensor.dtype),
            pltpu.VMEM((rank, width_y), y_factor.dtype),
            pltpu.VMEM(x_factor.shape, x_factor.dtype),
            pltpu.VMEM((width_x, depth * rank), jnp.float32),
            pltpu.VMEM((rank, depth * rank), jnp.float32),
            pltpu.SemaphoreType.DMA((depth + 2,)),
            pltpu.SemaphoreType.DMA((depth // 2, 2)),
        ],
        compiler_params=pltpu.CompilerParams(vmem_limit_bytes=56 * 2**20),
        name="projected",
    )(tensor, y_factor.T, x_factor)


def update_kernel(proj_ref, folded_ref, out_ref):
    n, half, lanes = out_ref.shape
    rank = lanes // 2
    part = lax.dot_general(
        proj_ref[...],
        folded_ref[...],
        (((1,), (1,)), ((), ())),
        precision=HIGHEST,
        preferred_element_type=jnp.float32,
    )
    part = part.reshape(n, 2, half, rank)
    out_ref[...] = jnp.concatenate([part[:, 0], part[:, 1]], axis=2)


def update_parts(proj_t, folded, n):
    width_x = proj_t.shape[0]
    rank = folded.shape[0]
    return pl.pallas_call(
        update_kernel,
        out_shape=jax.ShapeDtypeStruct((n, width_x // n // 2, 2 * rank), jnp.float32),
        in_specs=[ON_CHIP, ON_CHIP],
        out_specs=ON_CHIP,
        compiler_params=pltpu.CompilerParams(vmem_limit_bytes=24 * 2**20),
        name="update_parts",
    )(proj_t, folded)


def cross_kernel(parts_ref, update_ref, cross_ref):
    rank = update_ref.shape[1]
    packed = jnp.sum(parts_ref[...], axis=0)
    update_t = jnp.concatenate([packed[:, :rank], packed[:, rank:]], axis=0)
    update_ref[...] = update_t
    square = lax.dot_general(
        update_t,
        update_t,
        (((0,), (0,)), ((), ())),
        precision=HIGHEST,
        preferred_element_type=jnp.float32,
    )
    cross_ref[...] = jnp.concatenate([square[: rank // 2], square[rank // 2 :]], axis=1)


def own_update(parts):
    _, half, lanes = parts.shape
    rank = lanes // 2
    return pl.pallas_call(
        cross_kernel,
        out_shape=(
            jax.ShapeDtypeStruct((2 * half, rank), jnp.float32),
            jax.ShapeDtypeStruct((rank // 2, 2 * rank), jnp.float32),
        ),
        in_specs=[ON_CHIP],
        out_specs=(ON_CHIP, ON_CHIP),
        compiler_params=pltpu.CompilerParams(vmem_limit_bytes=8 * 2**20),
        name="own_update",
    )(parts)


def inverse_root(pivot):
    guess = lax.rsqrt(pivot)
    return guess * (1.5 - 0.5 * pivot * guess * guess)


def whitened_kernel(scale, cross_ref, update_ref, out_ref, aug, lanes):
    rank = update_ref.shape[1]
    cols = update_ref.shape[0]
    blocks = rank // 8
    wide = cross_ref[0]
    for i in range(1, cross_ref.shape[0]):
        wide = wide + cross_ref[i]
    gram = jnp.concatenate([wide[:, :rank], wide[:, rank:]], axis=0)
    padded = jnp.concatenate(
        [update_ref[...], jnp.zeros((rank - cols, rank), jnp.float32)], axis=0
    )
    aug[...] = jnp.concatenate([gram, padded.T], axis=1)
    rows = [aug[8 * i : 8 * i + 8, :] for i in range(blocks)]
    for j in range(blocks):
        aug[8 * j : 8 * j + 8, :] = rows[j]
        columns = []
        for i in range(j, blocks):
            columns.append(
                [
                    jnp.broadcast_to(rows[i][:, 8 * j + k : 8 * j + k + 1], (8, 128))
                    for k in range(8)
                ]
            )
        for k in range(8):
            lanes[8 * k : 8 * k + 8, :] = columns[0][k]
        a = [
            [jnp.broadcast_to(lanes[8 * k + m : 8 * k + m + 1, :], (8, 128)) for k in range(m + 1)]
            for m in range(8)
        ]
        right = [
            jnp.broadcast_to(aug[8 * j + k : 8 * j + k + 1, :], (8, 128)) for k in range(8)
        ]
        for k in range(8):
            root = inverse_root(a[k][k])
            for m in range(k + 1, 8):
                a[m][k] = a[m][k] * root
            right[k] = right[k] * root
            for column in columns[1:]:
                column[k] = column[k] * root
            for m in range(k + 1, 8):
                for n in range(k + 1, m + 1):
                    a[m][n] = a[m][n] - a[m][k] * a[n][k]
                right[m] = right[m] - a[m][k] * right[k]
                for column in columns[1:]:
                    column[m] = column[m] - column[k] * a[m][k]
        for k in range(8):
            aug[8 * j + k : 8 * j + k + 1, :] = right[k][:1]
        for i in range(j + 1, blocks):
            column = columns[i - j]
            first = column[0] * right[0] + column[1] * right[1]
            second = column[2] * right[2] + column[3] * right[3]
            third = column[4] * right[4] + column[5] * right[5]
            fourth = column[6] * right[6] + column[7] * right[7]
            rows[i] = rows[i] - ((first + second) + (third + fourth))
    out_ref[...] = aug[...].T[rank : rank + cols, :] * scale


def whitened(terms, update_t, scale):
    cols, rank = update_t.shape
    return pl.pallas_call(
        functools.partial(whitened_kernel, scale),
        out_shape=jax.ShapeDtypeStruct((cols, rank), jnp.float32),
        in_specs=[ON_CHIP, ON_CHIP],
        out_specs=ON_CHIP,
        scratch_shapes=[pltpu.VMEM((rank, 2 * rank), jnp.float32)] * 2,
        compiler_params=pltpu.CompilerParams(vmem_limit_bytes=8 * 2**20),
        name="whitened",
    )(terms, update_t)


def per_device(tensor, y_factor, x_factor):
    width_x = x_factor.shape[1]
    proj_t, folded_part = projected(tensor, y_factor, x_factor)
    folded = summed_everywhere(folded_part)
    parts = update_parts(proj_t, folded, lax.axis_size(GY))
    update_t, wide = own_update(exchanged(parts, GY))
    total_x = width_x * lax.axis_size(GX)
    return whitened(cross_terms(wide), update_t, float(total_x) ** 0.5).T


def solution(mesh):
    finer = Mesh(mesh.devices.reshape(2, 4, 2, 2, 8), AXES)
    in_specs = (P(None, GX, GY), P(GY, None), P(None, GX))
    out_specs = P(None, AXES)
    return jax.shard_map(
        per_device, mesh=finer, in_specs=in_specs, out_specs=out_specs, check_vma=False
    )
```

```python
import functools

import jax
import jax.numpy as jnp
from jax import lax
from jax.experimental import pallas as pl
from jax.experimental.pallas import tpu as pltpu
from jax.sharding import Mesh
from jax.sharding import PartitionSpec as P

AXES = ("y_lo", "x", "core", "y_hi", "z")
GX = ("y_lo", "x", "core")
GY = ("y_hi", "z")
CHIPS = ("y_hi", "y_lo", "x")
HIGHEST = lax.Precision.HIGHEST
ON_CHIP = pl.BlockSpec(memory_space=pltpu.VMEM)


def exchanged(tiles, axis):
    return lax.all_to_all(tiles, axis, 0, 0, tiled=True)


def of_everyone(tile, axis):
    return exchanged(jnp.broadcast_to(tile[None], (lax.axis_size(axis), *tile.shape)), axis)


def tiles_of(matrix):
    rows, cols = matrix.shape
    return matrix.reshape(rows // 8, 8, cols // 128, 128).swapaxes(1, 2).reshape(-1, 8, 128)


def from_tiles(tiles, rows, cols):
    return tiles.reshape(rows // 8, cols // 128, 8, 128).swapaxes(1, 2).reshape(rows, cols)


def summed_everywhere(matrix):
    rows, cols = matrix.shape
    tiles = tiles_of(matrix).reshape(lax.axis_size(GX), -1, 128)
    own = jnp.sum(exchanged(tiles, GX), axis=0)
    own = jnp.sum(of_everyone(own, GY), axis=0)
    return from_tiles(of_everyone(own, GX).reshape(-1, 8, 128), rows, cols)


def cross_terms(wide):
    wide = wide + lax.ppermute(wide, "core", [(0, 1), (1, 0)])
    wide = jnp.sum(of_everyone(wide, CHIPS), axis=0)
    return of_everyone(wide, "z")


def rounded_parts(matrix):
    high = matrix.astype(jnp.bfloat16)
    rest = matrix - high.astype(jnp.float32)
    middle = rest.astype(jnp.bfloat16)
    low = (rest - middle.astype(jnp.float32)).astype(jnp.bfloat16)
    return high, middle, low


def project_kernel(
    tensor_ref, y_ref, x_ref, kept_ref, sent_ref, folded_ref, planes, y_here, x_here, arrived
):
    depth = planes.shape[0]
    rank = y_ref.shape[0]
    y_copy = pltpu.make_async_copy(y_ref, y_here, arrived.at[depth])
    x_copy = pltpu.make_async_copy(x_ref, x_here, arrived.at[depth + 1])
    y_copy.start()

    def plane(z):
        return pltpu.make_async_copy(tensor_ref.at[z], planes.at[z], arrived.at[z])

    for z in range(depth):
        plane(z).start()
    x_copy.start()
    first = lax.axis_index("y_hi") == 0
    y_copy.wait()
    y_t = y_here[...]
    none = jnp.zeros_like(y_t)
    sides = (jnp.concatenate([y_t, none], axis=0), jnp.concatenate([none, y_t], axis=0))
    contract = (((1,), (1,)), ((), ()))
    for pair in range(depth // 2):
        total = None
        for side in range(2):
            z = 2 * pair + side
            plane(z).wait()
            term = lax.dot_general(
                planes[z], sides[side], contract, preferred_element_type=jnp.float32
            )
            total = term if total is None else total + term
        lanes = pl.ds(2 * rank * pair, 2 * rank)
        half = total.shape[0] // 2
        kept_ref[:, lanes] = jnp.where(first, total[:half], total[half:])
        sent_ref[:, lanes] = jnp.where(first, total[half:], total[:half])
        if pair == 0:
            x_copy.wait()
        folded = None
        for part in rounded_parts(total):
            term = jnp.dot(x_here[...], part, preferred_element_type=jnp.float32)
            folded = term if folded is None else folded + term
        folded_ref[:, lanes] = folded


def projected(tensor, y_factor, x_factor):
    depth, width_x, width_y = tensor.shape
    rank = y_factor.shape[1]
    return pl.pallas_call(
        project_kernel,
        out_shape=(
            jax.ShapeDtypeStruct((width_x // 2, depth * rank), jnp.float32),
            jax.ShapeDtypeStruct((width_x // 2, depth * rank), jnp.float32),
            jax.ShapeDtypeStruct((rank, depth * rank), jnp.float32),
        ),
        in_specs=[pl.BlockSpec(memory_space=pltpu.HBM)] * 3,
        out_specs=(ON_CHIP, ON_CHIP, ON_CHIP),
        scratch_shapes=[
            pltpu.VMEM(tensor.shape, tensor.dtype),
            pltpu.VMEM((rank, width_y), y_factor.dtype),
            pltpu.VMEM(x_factor.shape, x_factor.dtype),
            pltpu.SemaphoreType.DMA((depth + 2,)),
        ],
        compiler_params=pltpu.CompilerParams(vmem_limit_bytes=24 * 2**20),
        name="projected",
    )(*(pltpu.with_memory_space_constraint(a, pltpu.HBM) for a in (tensor, y_factor.T, x_factor)))


def update_kernel(kept_ref, come_ref, folded_ref, out_ref):
    n, half, lanes = out_ref.shape
    rank = lanes // 2
    part = lax.dot_general(
        kept_ref[...] + come_ref[...],
        folded_ref[...],
        (((1,), (1,)), ((), ())),
        precision=HIGHEST,
        preferred_element_type=jnp.float32,
    )
    part = part.reshape(n, 2, half, rank)
    out_ref[...] = jnp.concatenate([part[:, 0], part[:, 1]], axis=2)


def update_parts(kept, come, folded, n):
    width_x = kept.shape[0]
    rank = folded.shape[0]
    return pl.pallas_call(
        update_kernel,
        out_shape=jax.ShapeDtypeStruct((n, width_x // n // 2, 2 * rank), jnp.float32),
        in_specs=[ON_CHIP] * 3,
        out_specs=ON_CHIP,
        compiler_params=pltpu.CompilerParams(vmem_limit_bytes=24 * 2**20),
        name="update_parts",
    )(kept, come, folded)


def cross_kernel(parts_ref, update_ref, cross_ref):
    rank = update_ref.shape[1]
    packed = jnp.sum(parts_ref[...], axis=0)
    update_t = jnp.concatenate([packed[:, :rank], packed[:, rank:]], axis=0)
    update_ref[...] = update_t
    square = lax.dot_general(
        update_t,
        update_t,
        (((0,), (0,)), ((), ())),
        precision=HIGHEST,
        preferred_element_type=jnp.float32,
    )
    cross_ref[...] = jnp.concatenate([square[: rank // 2], square[rank // 2 :]], axis=1)


def own_update(parts):
    _, half, lanes = parts.shape
    rank = lanes // 2
    return pl.pallas_call(
        cross_kernel,
        out_shape=(
            jax.ShapeDtypeStruct((2 * half, rank), jnp.float32),
            jax.ShapeDtypeStruct((rank // 2, 2 * rank), jnp.float32),
        ),
        in_specs=[ON_CHIP],
        out_specs=(ON_CHIP, ON_CHIP),
        compiler_params=pltpu.CompilerParams(vmem_limit_bytes=8 * 2**20),
        name="own_update",
    )(parts)


def inverse_root(pivot):
    guess = lax.rsqrt(pivot)
    return guess * (1.5 - 0.5 * pivot * guess * guess)


def whitened_kernel(scale, cross_ref, update_ref, out_ref, aug, lanes):
    rank = update_ref.shape[1]
    cols = update_ref.shape[0]
    blocks = rank // 8
    wide = cross_ref[0]
    for i in range(1, cross_ref.shape[0]):
        wide = wide + cross_ref[i]
    gram = jnp.concatenate([wide[:, :rank], wide[:, rank:]], axis=0)
    padded = jnp.concatenate(
        [update_ref[...], jnp.zeros((rank - cols, rank), jnp.float32)], axis=0
    )
    aug[...] = jnp.concatenate([gram, padded.T], axis=1)
    rows = [aug[8 * i : 8 * i + 8, :] for i in range(blocks)]
    for j in range(blocks):
        aug[8 * j : 8 * j + 8, :] = rows[j]
        columns = []
        for i in range(j, blocks):
            columns.append(
                [
                    jnp.broadcast_to(rows[i][:, 8 * j + k : 8 * j + k + 1], (8, 128))
                    for k in range(8)
                ]
            )
        for k in range(8):
            lanes[8 * k : 8 * k + 8, :] = columns[0][k]
        a = [
            [jnp.broadcast_to(lanes[8 * k + m : 8 * k + m + 1, :], (8, 128)) for k in range(m + 1)]
            for m in range(8)
        ]
        right = [
            jnp.broadcast_to(aug[8 * j + k : 8 * j + k + 1, :], (8, 128)) for k in range(8)
        ]
        for k in range(8):
            root = inverse_root(a[k][k])
            for m in range(k + 1, 8):
                a[m][k] = a[m][k] * root
            right[k] = right[k] * root
            for column in columns[1:]:
                column[k] = column[k] * root
            for m in range(k + 1, 8):
                for n in range(k + 1, m + 1):
                    a[m][n] = a[m][n] - a[m][k] * a[n][k]
                right[m] = right[m] - a[m][k] * right[k]
                for column in columns[1:]:
                    column[m] = column[m] - column[k] * a[m][k]
        for k in range(8):
            aug[8 * j + k : 8 * j + k + 1, :] = right[k][:1]
        for i in range(j + 1, blocks):
            column = columns[i - j]
            first = column[0] * right[0] + column[1] * right[1]
            second = column[2] * right[2] + column[3] * right[3]
            third = column[4] * right[4] + column[5] * right[5]
            fourth = column[6] * right[6] + column[7] * right[7]
            rows[i] = rows[i] - ((first + second) + (third + fourth))
    out_ref[...] = aug[...].T[rank : rank + cols, :] * scale


def whitened(terms, update_t, scale):
    cols, rank = update_t.shape
    return pl.pallas_call(
        functools.partial(whitened_kernel, scale),
        out_shape=jax.ShapeDtypeStruct((cols, rank), jnp.float32),
        in_specs=[ON_CHIP, ON_CHIP],
        out_specs=ON_CHIP,
        scratch_shapes=[pltpu.VMEM((rank, 2 * rank), jnp.float32)] * 2,
        compiler_params=pltpu.CompilerParams(vmem_limit_bytes=8 * 2**20),
        name="whitened",
    )(terms, update_t)


def per_device(tensor, y_factor, x_factor):
    width_x = x_factor.shape[1]
    kept, sent, folded_part = projected(tensor, y_factor, x_factor)
    come = lax.ppermute(sent, "y_hi", [(0, 1), (1, 0)])
    folded = summed_everywhere(folded_part)
    parts = update_parts(kept, come, folded, lax.axis_size("z"))
    update_t, wide = own_update(exchanged(parts, "z"))
    total_x = width_x * lax.axis_size(GX)
    return whitened(cross_terms(wide), update_t, float(total_x) ** 0.5).T


def solution(mesh):
    finer = Mesh(mesh.devices.reshape(2, 4, 2, 2, 8), AXES)
    in_specs = (P(None, GX, GY), P(GY, None), P(None, GX))
    out_specs = P(None, AXES)
    return jax.shard_map(
        per_device, mesh=finer, in_specs=in_specs, out_specs=out_specs, check_vma=False
    )
```

```python
import functools

import jax
import jax.numpy as jnp
from jax import lax
from jax.experimental import pallas as pl
from jax.experimental.pallas import tpu as pltpu
from jax.sharding import Mesh
from jax.sharding import PartitionSpec as P

AXES = ("y_lo", "x", "core", "y_hi", "z")
GX = ("y_lo", "x", "core")
GY = ("y_hi", "z")
PLANE = ("y_hi", "y_lo", "x", "core")
CHIPS = ("y_hi", "y_lo", "x")
HIGHEST = lax.Precision.HIGHEST
ON_CHIP = pl.BlockSpec(memory_space=pltpu.VMEM)


def exchanged(tiles, axis):
    return lax.all_to_all(tiles, axis, 0, 0, tiled=True)


def of_everyone(tile, axis):
    return exchanged(jnp.broadcast_to(tile[None], (lax.axis_size(axis), *tile.shape)), axis)


def tiles_of(matrix):
    rows, cols = matrix.shape
    return matrix.reshape(rows // 8, 8, cols // 128, 128).swapaxes(1, 2).reshape(-1, 8, 128)


def from_tiles(tiles, rows, cols):
    return tiles.reshape(rows // 8, cols // 128, 8, 128).swapaxes(1, 2).reshape(rows, cols)


def summed_everywhere(matrix, sent):
    rows, cols = matrix.shape
    tiles = tiles_of(matrix).reshape(lax.axis_size(PLANE), -1, 128)
    own = jnp.sum(exchanged(tiles, PLANE), axis=0)
    own, sent = lax.optimization_barrier((own, sent))
    come = lax.ppermute(sent, "y_hi", [(0, 1), (1, 0)])
    own = jnp.sum(of_everyone(own, "z"), axis=0)
    everything = of_everyone(own, PLANE).reshape(-1, 8, 128)
    return from_tiles(everything, rows, cols), come


def with_neighbour(value, axis):
    pairs = [(i, i ^ 1) for i in range(lax.axis_size(axis))]
    return value + lax.ppermute(value, axis, pairs)


def rounded_parts(matrix):
    high = matrix.astype(jnp.bfloat16)
    rest = matrix - high.astype(jnp.float32)
    middle = rest.astype(jnp.bfloat16)
    low = (rest - middle.astype(jnp.float32)).astype(jnp.bfloat16)
    return high, middle, low


def project_kernel(
    tensor_ref, y_ref, x_ref, kept_ref, sent_ref, folded_ref, planes, y_here, x_here, arrived
):
    depth = planes.shape[0]
    rank = y_ref.shape[0]
    y_copy = pltpu.make_async_copy(y_ref, y_here, arrived.at[depth])
    x_copy = pltpu.make_async_copy(x_ref, x_here, arrived.at[depth + 1])
    y_copy.start()

    def plane(z):
        return pltpu.make_async_copy(tensor_ref.at[z], planes.at[z], arrived.at[z])

    for z in range(depth):
        plane(z).start()
    x_copy.start()
    first = lax.axis_index("y_hi") == 0
    y_copy.wait()
    y_t = y_here[...]
    none = jnp.zeros_like(y_t)
    sides = (jnp.concatenate([y_t, none], axis=0), jnp.concatenate([none, y_t], axis=0))
    contract = (((1,), (1,)), ((), ()))
    for pair in range(depth // 2):
        total = None
        for side in range(2):
            z = 2 * pair + side
            plane(z).wait()
            term = lax.dot_general(
                planes[z], sides[side], contract, preferred_element_type=jnp.float32
            )
            total = term if total is None else total + term
        lanes = pl.ds(2 * rank * pair, 2 * rank)
        half = total.shape[0] // 2
        kept_ref[:, lanes] = jnp.where(first, total[:half], total[half:])
        sent_ref[:, lanes] = jnp.where(first, total[half:], total[:half])
        if pair == 0:
            x_copy.wait()
        folded = None
        for part in rounded_parts(total):
            term = jnp.dot(x_here[...], part, preferred_element_type=jnp.float32)
            folded = term if folded is None else folded + term
        folded_ref[:, lanes] = folded


def projected(tensor, y_factor, x_factor):
    depth, width_x, width_y = tensor.shape
    rank = y_factor.shape[1]
    return pl.pallas_call(
        project_kernel,
        out_shape=(
            jax.ShapeDtypeStruct((width_x // 2, depth * rank), jnp.float32),
            jax.ShapeDtypeStruct((width_x // 2, depth * rank), jnp.float32),
            jax.ShapeDtypeStruct((rank, depth * rank), jnp.float32),
        ),
        in_specs=[pl.BlockSpec(memory_space=pltpu.HBM)] * 3,
        out_specs=(ON_CHIP, ON_CHIP, ON_CHIP),
        scratch_shapes=[
            pltpu.VMEM(tensor.shape, tensor.dtype),
            pltpu.VMEM((rank, width_y), y_factor.dtype),
            pltpu.VMEM(x_factor.shape, x_factor.dtype),
            pltpu.SemaphoreType.DMA((depth + 2,)),
        ],
        compiler_params=pltpu.CompilerParams(vmem_limit_bytes=24 * 2**20),
        name="projected",
    )(*(pltpu.with_memory_space_constraint(a, pltpu.HBM) for a in (tensor, y_factor.T, x_factor)))


def update_kernel(kept_ref, come_ref, folded_ref, out_ref):
    n, rows, lanes = out_ref.shape
    rank = lanes // 2
    half = 2 * rows // n
    part = lax.dot_general(
        kept_ref[...] + come_ref[...],
        folded_ref[...],
        (((1,), (1,)), ((), ())),
        precision=HIGHEST,
        preferred_element_type=jnp.float32,
    )
    part = part.reshape(n, 2, half, rank)
    packed = jnp.concatenate([part[:, 0], part[:, 1]], axis=2)
    packed = packed.reshape(n // 2, 2, half, lanes)
    for z in range(n):
        out_ref[z] = packed[:, z % 2].reshape(rows, lanes)


def update_parts(kept, come, folded, n):
    width_x = kept.shape[0]
    rank = folded.shape[0]
    return pl.pallas_call(
        update_kernel,
        out_shape=jax.ShapeDtypeStruct((n, width_x // 4, 2 * rank), jnp.float32),
        in_specs=[ON_CHIP] * 3,
        out_specs=ON_CHIP,
        compiler_params=pltpu.CompilerParams(vmem_limit_bytes=24 * 2**20),
        name="update_parts",
    )(kept, come, folded)


def cross_kernel(parts_ref, update_ref, cross_ref, packed_ref):
    rank = update_ref.shape[1]
    half = update_ref.shape[0] // 2
    packed = jnp.sum(parts_ref[...], axis=0)
    packed_ref[...] = packed
    update_t = jnp.concatenate([packed[:, :rank], packed[:, rank:]], axis=0)
    square = lax.dot_general(
        update_t,
        update_t,
        (((0,), (0,)), ((), ())),
        precision=HIGHEST,
        preferred_element_type=jnp.float32,
    )
    cross_ref[...] = jnp.concatenate([square[: rank // 2], square[rank // 2 :]], axis=1)
    start = pl.multiple_of(lax.axis_index("z") // 2 * half, half)
    own = packed_ref[pl.ds(start, half), :]
    update_ref[...] = jnp.concatenate([own[:, :rank], own[:, rank:]], axis=0)


def own_update(parts):
    n, rows, lanes = parts.shape
    rank = lanes // 2
    return pl.pallas_call(
        cross_kernel,
        out_shape=(
            jax.ShapeDtypeStruct((4 * rows // n, rank), jnp.float32),
            jax.ShapeDtypeStruct((rank // 2, 2 * rank), jnp.float32),
        ),
        in_specs=[ON_CHIP],
        out_specs=(ON_CHIP, ON_CHIP),
        scratch_shapes=[pltpu.VMEM((rows, lanes), jnp.float32)],
        compiler_params=pltpu.CompilerParams(vmem_limit_bytes=8 * 2**20),
        name="own_update",
    )(parts)


def inverse_root(pivot):
    guess = lax.rsqrt(pivot)
    return guess * (1.5 - 0.5 * pivot * guess * guess)


def whitened_kernel(scale, cross_ref, update_ref, out_ref, aug, lanes):
    rank = update_ref.shape[1]
    cols = update_ref.shape[0]
    blocks = rank // 8
    wide = cross_ref[0]
    for i in range(1, cross_ref.shape[0]):
        wide = wide + cross_ref[i]
    gram = jnp.concatenate([wide[:, :rank], wide[:, rank:]], axis=0)
    padded = jnp.concatenate(
        [update_ref[...], jnp.zeros((rank - cols, rank), jnp.float32)], axis=0
    )
    aug[...] = jnp.concatenate([gram, padded.T], axis=1)
    rows = [aug[8 * i : 8 * i + 8, :] for i in range(blocks)]
    for j in range(blocks):
        aug[8 * j : 8 * j + 8, :] = rows[j]
        columns = []
        for i in range(j, blocks):
            columns.append(
                [
                    jnp.broadcast_to(rows[i][:, 8 * j + k : 8 * j + k + 1], (8, 128))
                    for k in range(8)
                ]
            )
        for k in range(8):
            lanes[8 * k : 8 * k + 8, :] = columns[0][k]
        a = [
            [jnp.broadcast_to(lanes[8 * k + m : 8 * k + m + 1, :], (8, 128)) for k in range(m + 1)]
            for m in range(8)
        ]
        right = [
            jnp.broadcast_to(aug[8 * j + k : 8 * j + k + 1, :], (8, 128)) for k in range(8)
        ]
        for k in range(8):
            root = inverse_root(a[k][k])
            for m in range(k + 1, 8):
                a[m][k] = a[m][k] * root
            right[k] = right[k] * root
            for column in columns[1:]:
                column[k] = column[k] * root
            for m in range(k + 1, 8):
                for n in range(k + 1, m + 1):
                    a[m][n] = a[m][n] - a[m][k] * a[n][k]
                right[m] = right[m] - a[m][k] * right[k]
                for column in columns[1:]:
                    column[m] = column[m] - column[k] * a[m][k]
        for k in range(8):
            aug[8 * j + k : 8 * j + k + 1, :] = right[k][:1]
        for i in range(j + 1, blocks):
            column = columns[i - j]
            first = column[0] * right[0] + column[1] * right[1]
            second = column[2] * right[2] + column[3] * right[3]
            third = column[4] * right[4] + column[5] * right[5]
            fourth = column[6] * right[6] + column[7] * right[7]
            rows[i] = rows[i] - ((first + second) + (third + fourth))
    out_ref[...] = aug[...].T[rank : rank + cols, :] * scale


def whitened(terms, update_t, scale):
    cols, rank = update_t.shape
    return pl.pallas_call(
        functools.partial(whitened_kernel, scale),
        out_shape=jax.ShapeDtypeStruct((cols, rank), jnp.float32),
        in_specs=[ON_CHIP, ON_CHIP],
        out_specs=ON_CHIP,
        scratch_shapes=[pltpu.VMEM((rank, 2 * rank), jnp.float32)] * 2,
        compiler_params=pltpu.CompilerParams(vmem_limit_bytes=8 * 2**20),
        name="whitened",
    )(terms, update_t)


def per_device(tensor, y_factor, x_factor):
    width_x = x_factor.shape[1]
    kept, sent, folded_part = projected(tensor, y_factor, x_factor)
    folded, come = summed_everywhere(folded_part, sent)
    parts = update_parts(kept, come, folded, lax.axis_size("z"))
    update_t, wide = own_update(exchanged(parts, "z"))
    wide = with_neighbour(with_neighbour(wide, "core"), "z")
    total_x = width_x * lax.axis_size(GX)
    return whitened(of_everyone(wide, CHIPS), update_t, float(total_x) ** 0.5).T


def solution(mesh):
    finer = Mesh(mesh.devices.reshape(2, 4, 2, 2, 8), AXES)
    in_specs = (P(None, GX, GY), P(GY, None), P(None, GX))
    out_specs = P(None, AXES)
    return jax.shard_map(
        per_device, mesh=finer, in_specs=in_specs, out_specs=out_specs, check_vma=False
    )
```

```python
import functools

import jax
import jax.numpy as jnp
from jax import lax
from jax.experimental import pallas as pl
from jax.experimental.pallas import tpu as pltpu
from jax.sharding import Mesh
from jax.sharding import PartitionSpec as P

AXES = ("y_lo", "x", "core", "y_hi", "z")
GX = ("y_lo", "x", "core")
GY = ("y_hi", "z")
CHIPS = ("y_hi", "y_lo", "x")
HIGHEST = lax.Precision.HIGHEST
EARLY = 6
ON_CHIP = pl.BlockSpec(memory_space=pltpu.VMEM)


def exchanged(tiles, axis):
    return lax.all_to_all(tiles, axis, 0, 0, tiled=True)


def of_everyone(tile, axis):
    return exchanged(jnp.broadcast_to(tile[None], (lax.axis_size(axis), *tile.shape)), axis)


def tiles_of(matrix):
    rows, cols = matrix.shape
    return matrix.reshape(rows // 8, 8, cols // 128, 128).swapaxes(1, 2).reshape(-1, 8, 128)


def from_tiles(tiles, rows, cols):
    return tiles.reshape(rows // 8, cols // 128, 8, 128).swapaxes(1, 2).reshape(rows, cols)


def from_partner(array, axis):
    return lax.ppermute(array, axis, [(i, i ^ 1) for i in range(lax.axis_size(axis))])


def summed_everywhere(own, other, sent):
    rows, cols = own.shape
    own = own + from_partner(other, "core")
    tiles = tiles_of(own).reshape(lax.axis_size(CHIPS), -1, 128)
    tile = jnp.sum(exchanged(tiles, CHIPS), axis=0)
    tile, sent = lax.optimization_barrier((tile, sent))
    come = from_partner(sent, "y_hi")
    tile = jnp.sum(of_everyone(tile, "z"), axis=0)
    own = from_tiles(of_everyone(tile, CHIPS).reshape(-1, 8, 128), rows, cols)
    return own, from_partner(own, "core"), come


def with_neighbour(value, axis):
    return value + from_partner(value, axis)


def rounded_parts(matrix):
    high = matrix.astype(jnp.bfloat16)
    rest = matrix - high.astype(jnp.float32)
    middle = rest.astype(jnp.bfloat16)
    low = (rest - middle.astype(jnp.float32)).astype(jnp.bfloat16)
    return high, middle, low


def project_kernel(
    tensor_ref,
    y_ref,
    x_ref,
    kept_ref,
    sent_ref,
    own_ref,
    other_ref,
    planes,
    y_here,
    x_here,
    arrived,
):
    depth, width_x, _ = planes.shape
    rank = y_ref.shape[0]
    half = width_x // 2
    y_copy = pltpu.make_async_copy(y_ref, y_here, arrived.at[depth])
    x_copy = pltpu.make_async_copy(x_ref, x_here, arrived.at[depth + 1])
    y_copy.start()

    def plane(z):
        return pltpu.make_async_copy(tensor_ref.at[z], planes.at[z], arrived.at[z])

    for z in range(EARLY):
        plane(z).start()
    x_copy.start()
    kept_at = pl.multiple_of(lax.axis_index("y_hi") * half, half)
    sides = ((kept_ref, kept_at), (sent_ref, pl.multiple_of(half - kept_at, half)))
    first = lax.axis_index("core") == 0
    y_copy.wait()
    y_t = y_here[...]
    none = jnp.zeros_like(y_t)
    y_left, y_right = jnp.concatenate([y_t, none], axis=0), jnp.concatenate([none, y_t], axis=0)
    contract = (((1,), (1,)), ((), ()))
    pairs = depth // 2
    for step in range(pairs + 1):
        if step < pairs:
            plane(2 * step).wait()
            plane(2 * step + 1).wait()
            for z in range(2 * step + EARLY, min(2 * step + EARLY + 2, depth)):
                plane(z).start()
        if step == 1:
            x_copy.wait()
        folded = None
        for there, start in sides:
            if step < pairs:
                rows = pl.ds(start, half)
                left = lax.dot_general(
                    planes[2 * step, rows, :], y_left, contract, preferred_element_type=jnp.float32
                )
                right = lax.dot_general(
                    planes[2 * step + 1, rows, :],
                    y_right,
                    contract,
                    preferred_element_type=jnp.float32,
                )
                there[:, pl.ds(2 * rank * step, 2 * rank)] = left + right
            if step > 0:
                x_part = x_here[:, pl.ds(start, half)]
                for part in rounded_parts(there[:, pl.ds(2 * rank * (step - 1), 2 * rank)]):
                    term = jnp.dot(x_part, part, preferred_element_type=jnp.float32)
                    folded = term if folded is None else folded + term
        if step > 0:
            lanes = pl.ds(2 * rank * (step - 1), 2 * rank)
            upper, lower = folded[: rank // 2], folded[rank // 2 :]
            own_ref[:, lanes] = jnp.where(first, upper, lower)
            other_ref[:, lanes] = jnp.where(first, lower, upper)


def projected(tensor, y_factor, x_factor):
    depth, width_x, width_y = tensor.shape
    rank = y_factor.shape[1]
    rows = depth * rank
    return pl.pallas_call(
        project_kernel,
        out_shape=[
            jax.ShapeDtypeStruct((n, rows), jnp.float32)
            for n in (width_x // 2, width_x // 2, rank // 2, rank // 2)
        ],
        in_specs=[pl.BlockSpec(memory_space=pltpu.HBM)] * 3,
        out_specs=[ON_CHIP] * 4,
        scratch_shapes=[
            pltpu.VMEM(tensor.shape, tensor.dtype),
            pltpu.VMEM((rank, width_y), y_factor.dtype),
            pltpu.VMEM(x_factor.shape, x_factor.dtype),
            pltpu.SemaphoreType.DMA((depth + 2,)),
        ],
        compiler_params=pltpu.CompilerParams(vmem_limit_bytes=24 * 2**20),
        name="projected",
    )(*(pltpu.with_memory_space_constraint(a, pltpu.HBM) for a in (tensor, y_factor.T, x_factor)))


def update_kernel(kept_ref, come_ref, own_ref, other_ref, out_ref):
    n, rows, lanes = out_ref.shape
    rank = lanes // 2
    half = 2 * rows // n
    first = lax.axis_index("core") == 0
    own, other = own_ref[...], other_ref[...]
    folded = jnp.concatenate([jnp.where(first, own, other), jnp.where(first, other, own)], axis=0)
    part = lax.dot_general(
        kept_ref[...] + come_ref[...],
        folded,
        (((1,), (1,)), ((), ())),
        precision=HIGHEST,
        preferred_element_type=jnp.float32,
    )
    part = part.reshape(n, 2, half, rank)
    packed = jnp.concatenate([part[:, 0], part[:, 1]], axis=2)
    packed = packed.reshape(n // 2, 2, half, lanes)
    for z in range(n):
        out_ref[z] = packed[:, z % 2].reshape(rows, lanes)


def update_parts(kept, come, own, other, n):
    width_x = kept.shape[0]
    rank = 2 * own.shape[0]
    return pl.pallas_call(
        update_kernel,
        out_shape=jax.ShapeDtypeStruct((n, width_x // 4, 2 * rank), jnp.float32),
        in_specs=[ON_CHIP] * 4,
        out_specs=ON_CHIP,
        compiler_params=pltpu.CompilerParams(vmem_limit_bytes=24 * 2**20),
        name="update_parts",
    )(kept, come, own, other)


def cross_kernel(parts_ref, update_ref, cross_ref, packed_ref):
    rank = update_ref.shape[1]
    half = update_ref.shape[0] // 2
    packed = jnp.sum(parts_ref[...], axis=0)
    packed_ref[...] = packed
    update_t = jnp.concatenate([packed[:, :rank], packed[:, rank:]], axis=0)
    square = lax.dot_general(
        update_t,
        update_t,
        (((0,), (0,)), ((), ())),
        precision=HIGHEST,
        preferred_element_type=jnp.float32,
    )
    cross_ref[...] = jnp.concatenate([square[: rank // 2], square[rank // 2 :]], axis=1)
    start = pl.multiple_of(lax.axis_index("z") // 2 * half, half)
    own = packed_ref[pl.ds(start, half), :]
    update_ref[...] = jnp.concatenate([own[:, :rank], own[:, rank:]], axis=0)


def own_update(parts):
    n, rows, lanes = parts.shape
    rank = lanes // 2
    return pl.pallas_call(
        cross_kernel,
        out_shape=(
            jax.ShapeDtypeStruct((4 * rows // n, rank), jnp.float32),
            jax.ShapeDtypeStruct((rank // 2, 2 * rank), jnp.float32),
        ),
        in_specs=[ON_CHIP],
        out_specs=(ON_CHIP, ON_CHIP),
        scratch_shapes=[pltpu.VMEM((rows, lanes), jnp.float32)],
        compiler_params=pltpu.CompilerParams(vmem_limit_bytes=8 * 2**20),
        name="own_update",
    )(parts)


def inverse_root(pivot):
    guess = lax.rsqrt(pivot)
    return guess * (1.5 - 0.5 * pivot * guess * guess)


def whitened_kernel(scale, cross_ref, update_ref, out_ref, aug, lanes):
    rank = update_ref.shape[1]
    cols = update_ref.shape[0]
    blocks = rank // 8
    wide = cross_ref[0]
    for i in range(1, cross_ref.shape[0]):
        wide = wide + cross_ref[i]
    gram = jnp.concatenate([wide[:, :rank], wide[:, rank:]], axis=0)
    padded = jnp.concatenate(
        [update_ref[...], jnp.zeros((rank - cols, rank), jnp.float32)], axis=0
    )
    aug[...] = jnp.concatenate([gram, padded.T], axis=1)
    rows = [aug[8 * i : 8 * i + 8, :] for i in range(blocks)]
    for j in range(blocks):
        aug[8 * j : 8 * j + 8, :] = rows[j]
        columns = []
        for i in range(j, blocks):
            columns.append(
                [
                    jnp.broadcast_to(rows[i][:, 8 * j + k : 8 * j + k + 1], (8, 128))
                    for k in range(8)
                ]
            )
        for k in range(8):
            lanes[8 * k : 8 * k + 8, :] = columns[0][k]
        a = [
            [jnp.broadcast_to(lanes[8 * k + m : 8 * k + m + 1, :], (8, 128)) for k in range(m + 1)]
            for m in range(8)
        ]
        right = [
            jnp.broadcast_to(aug[8 * j + k : 8 * j + k + 1, :], (8, 128)) for k in range(8)
        ]
        for k in range(8):
            root = inverse_root(a[k][k])
            for m in range(k + 1, 8):
                a[m][k] = a[m][k] * root
            right[k] = right[k] * root
            for column in columns[1:]:
                column[k] = column[k] * root
            for m in range(k + 1, 8):
                for n in range(k + 1, m + 1):
                    a[m][n] = a[m][n] - a[m][k] * a[n][k]
                right[m] = right[m] - a[m][k] * right[k]
                for column in columns[1:]:
                    column[m] = column[m] - column[k] * a[m][k]
        for k in range(8):
            aug[8 * j + k : 8 * j + k + 1, :] = right[k][:1]
        for i in range(j + 1, blocks):
            column = columns[i - j]
            first = column[0] * right[0] + column[1] * right[1]
            second = column[2] * right[2] + column[3] * right[3]
            third = column[4] * right[4] + column[5] * right[5]
            fourth = column[6] * right[6] + column[7] * right[7]
            rows[i] = rows[i] - ((first + second) + (third + fourth))
    out_ref[...] = aug[...].T[rank : rank + cols, :] * scale


def whitened(terms, update_t, scale):
    cols, rank = update_t.shape
    return pl.pallas_call(
        functools.partial(whitened_kernel, scale),
        out_shape=jax.ShapeDtypeStruct((cols, rank), jnp.float32),
        in_specs=[ON_CHIP, ON_CHIP],
        out_specs=ON_CHIP,
        scratch_shapes=[pltpu.VMEM((rank, 2 * rank), jnp.float32)] * 2,
        compiler_params=pltpu.CompilerParams(vmem_limit_bytes=8 * 2**20),
        name="whitened",
    )(terms, update_t)


def per_device(tensor, y_factor, x_factor):
    width_x = x_factor.shape[1]
    kept, sent, own, other = projected(tensor, y_factor, x_factor)
    own, other, come = summed_everywhere(own, other, sent)
    parts = update_parts(kept, come, own, other, lax.axis_size("z"))
    update_t, wide = own_update(exchanged(parts, "z"))
    wide = with_neighbour(with_neighbour(wide, "core"), "z")
    total_x = width_x * lax.axis_size(GX)
    return whitened(of_everyone(wide, CHIPS), update_t, float(total_x) ** 0.5).T


def solution(mesh):
    finer = Mesh(mesh.devices.reshape(2, 4, 2, 2, 8), AXES)
    in_specs = (P(None, GX, GY), P(GY, None), P(None, GX))
    out_specs = P(None, AXES)
    return jax.shard_map(
        per_device, mesh=finer, in_specs=in_specs, out_specs=out_specs, check_vma=False
    )
```

```python
import functools

import jax
import jax.numpy as jnp
from jax import lax
from jax.experimental import pallas as pl
from jax.experimental.pallas import tpu as pltpu
from jax.sharding import Mesh
from jax.sharding import PartitionSpec as P

AXES = ("y_lo", "x", "core", "y_hi", "z")
GX = ("y_lo", "x", "core")
GY = ("y_hi", "z")
PLANE = ("y_hi", "y_lo", "x", "core")
CHIPS = ("y_hi", "y_lo", "x")
HIGHEST = lax.Precision.HIGHEST
EARLY = 6
ON_CHIP = pl.BlockSpec(memory_space=pltpu.VMEM)


def exchanged(tiles, axis):
    return lax.all_to_all(tiles, axis, 0, 0, tiled=True)


def of_everyone(tile, axis):
    return exchanged(jnp.broadcast_to(tile[None], (lax.axis_size(axis), *tile.shape)), axis)


def tiles_of(matrix):
    rows, cols = matrix.shape
    return matrix.reshape(rows // 8, 8, cols // 128, 128).swapaxes(1, 2).reshape(-1, 8, 128)


def from_tiles(tiles, rows, cols):
    return tiles.reshape(rows // 8, cols // 128, 8, 128).swapaxes(1, 2).reshape(rows, cols)


def from_partner(array, axis):
    return lax.ppermute(array, axis, [(i, i ^ 1) for i in range(lax.axis_size(axis))])


def summed_everywhere(matrix, sent):
    rows, cols = matrix.shape
    chips, cores = lax.axis_size(CHIPS), lax.axis_size("core")
    tiles = tiles_of(matrix).reshape(chips, 1, -1, 128)
    tiles = jnp.broadcast_to(tiles, (chips, cores, *tiles.shape[2:]))
    own = jnp.sum(exchanged(tiles.reshape(chips * cores, -1, 128), PLANE), axis=0)
    own, sent = lax.optimization_barrier((own, sent))
    come = from_partner(sent, "y_hi")
    own = jnp.sum(of_everyone(own, "z"), axis=0)
    return from_tiles(of_everyone(own, CHIPS).reshape(-1, 8, 128), rows, cols), come


def with_neighbour(value, axis):
    return value + from_partner(value, axis)


def rounded_parts(matrix):
    high = matrix.astype(jnp.bfloat16)
    rest = matrix - high.astype(jnp.float32)
    middle = rest.astype(jnp.bfloat16)
    low = (rest - middle.astype(jnp.float32)).astype(jnp.bfloat16)
    return high, middle, low


def project_kernel(
    tensor_ref,
    y_ref,
    x_ref,
    kept_ref,
    sent_ref,
    folded_ref,
    planes,
    y_here,
    x_here,
    arrived,
):
    depth, width_x, _ = planes.shape
    rank = y_ref.shape[0]
    half = width_x // 2
    y_copy = pltpu.make_async_copy(y_ref, y_here, arrived.at[depth])
    x_copy = pltpu.make_async_copy(x_ref, x_here, arrived.at[depth + 1])
    y_copy.start()

    def plane(z):
        return pltpu.make_async_copy(tensor_ref.at[z], planes.at[z], arrived.at[z])

    for z in range(EARLY):
        plane(z).start()
    x_copy.start()
    kept_at = pl.multiple_of(lax.axis_index("y_hi") * half, half)
    sides = ((kept_ref, kept_at), (sent_ref, pl.multiple_of(half - kept_at, half)))
    y_copy.wait()
    y_t = y_here[...]
    none = jnp.zeros_like(y_t)
    y_left, y_right = jnp.concatenate([y_t, none], axis=0), jnp.concatenate([none, y_t], axis=0)
    contract = (((1,), (1,)), ((), ()))
    pairs = depth // 2
    for step in range(pairs + 1):
        if step < pairs:
            plane(2 * step).wait()
            plane(2 * step + 1).wait()
            for z in range(2 * step + EARLY, min(2 * step + EARLY + 2, depth)):
                plane(z).start()
        if step == 1:
            x_copy.wait()
        folded = None
        for there, start in sides:
            if step < pairs:
                rows = pl.ds(start, half)
                left = lax.dot_general(
                    planes[2 * step, rows, :], y_left, contract, preferred_element_type=jnp.float32
                )
                right = lax.dot_general(
                    planes[2 * step + 1, rows, :],
                    y_right,
                    contract,
                    preferred_element_type=jnp.float32,
                )
                there[:, pl.ds(2 * rank * step, 2 * rank)] = left + right
            if step > 0:
                x_part = x_here[:, pl.ds(start, half)]
                for part in rounded_parts(there[:, pl.ds(2 * rank * (step - 1), 2 * rank)]):
                    term = jnp.dot(x_part, part, preferred_element_type=jnp.float32)
                    folded = term if folded is None else folded + term
        if step > 0:
            folded_ref[:, pl.ds(2 * rank * (step - 1), 2 * rank)] = folded


def projected(tensor, y_factor, x_factor):
    depth, width_x, width_y = tensor.shape
    rank = y_factor.shape[1]
    rows = depth * rank
    return pl.pallas_call(
        project_kernel,
        out_shape=[
            jax.ShapeDtypeStruct((n, rows), jnp.float32)
            for n in (width_x // 2, width_x // 2, rank)
        ],
        in_specs=[pl.BlockSpec(memory_space=pltpu.HBM)] * 3,
        out_specs=[ON_CHIP] * 3,
        scratch_shapes=[
            pltpu.VMEM(tensor.shape, tensor.dtype),
            pltpu.VMEM((rank, width_y), y_factor.dtype),
            pltpu.VMEM(x_factor.shape, x_factor.dtype),
            pltpu.SemaphoreType.DMA((depth + 2,)),
        ],
        compiler_params=pltpu.CompilerParams(vmem_limit_bytes=24 * 2**20),
        name="projected",
    )(*(pltpu.with_memory_space_constraint(a, pltpu.HBM) for a in (tensor, y_factor.T, x_factor)))


def update_kernel(kept_ref, come_ref, folded_ref, out_ref):
    n, rows, lanes = out_ref.shape
    rank = lanes // 2
    half = 2 * rows // n
    part = lax.dot_general(
        kept_ref[...] + come_ref[...],
        folded_ref[...],
        (((1,), (1,)), ((), ())),
        precision=HIGHEST,
        preferred_element_type=jnp.float32,
    )
    part = part.reshape(n, 2, half, rank)
    packed = jnp.concatenate([part[:, 0], part[:, 1]], axis=2)
    packed = packed.reshape(n // 2, 2, half, lanes)
    for z in range(n):
        out_ref[z] = packed[:, z % 2].reshape(rows, lanes)


def update_parts(kept, come, folded, n):
    width_x = kept.shape[0]
    rank = folded.shape[0]
    return pl.pallas_call(
        update_kernel,
        out_shape=jax.ShapeDtypeStruct((n, width_x // 4, 2 * rank), jnp.float32),
        in_specs=[ON_CHIP] * 3,
        out_specs=ON_CHIP,
        compiler_params=pltpu.CompilerParams(vmem_limit_bytes=24 * 2**20),
        name="update_parts",
    )(kept, come, folded)


def cross_kernel(parts_ref, update_ref, cross_ref, packed_ref):
    rank = update_ref.shape[1]
    half = update_ref.shape[0] // 2
    packed = jnp.sum(parts_ref[...], axis=0)
    packed_ref[...] = packed
    update_t = jnp.concatenate([packed[:, :rank], packed[:, rank:]], axis=0)
    square = lax.dot_general(
        update_t,
        update_t,
        (((0,), (0,)), ((), ())),
        precision=HIGHEST,
        preferred_element_type=jnp.float32,
    )
    cross_ref[...] = jnp.concatenate([square[: rank // 2], square[rank // 2 :]], axis=1)
    start = pl.multiple_of(lax.axis_index("z") // 2 * half, half)
    own = packed_ref[pl.ds(start, half), :]
    update_ref[...] = jnp.concatenate([own[:, :rank], own[:, rank:]], axis=0)


def own_update(parts):
    n, rows, lanes = parts.shape
    rank = lanes // 2
    return pl.pallas_call(
        cross_kernel,
        out_shape=(
            jax.ShapeDtypeStruct((4 * rows // n, rank), jnp.float32),
            jax.ShapeDtypeStruct((rank // 2, 2 * rank), jnp.float32),
        ),
        in_specs=[ON_CHIP],
        out_specs=(ON_CHIP, ON_CHIP),
        scratch_shapes=[pltpu.VMEM((rows, lanes), jnp.float32)],
        compiler_params=pltpu.CompilerParams(vmem_limit_bytes=8 * 2**20),
        name="own_update",
    )(parts)


def whitened_kernel(scale, cross_ref, update_ref, out_ref, aug, lanes):
    rank = update_ref.shape[1]
    cols = update_ref.shape[0]
    blocks = rank // 8
    wide = cross_ref[0]
    for i in range(1, cross_ref.shape[0]):
        wide = wide + cross_ref[i]
    gram = jnp.concatenate([wide[:, :rank], wide[:, rank:]], axis=0)
    padded = jnp.concatenate(
        [update_ref[...], jnp.zeros((rank - cols, rank), jnp.float32)], axis=0
    )
    aug[...] = jnp.concatenate([gram, padded.T], axis=1)
    rows = [aug[8 * i : 8 * i + 8, :] for i in range(blocks)]
    for j in range(blocks):
        aug[8 * j : 8 * j + 8, :] = rows[j]
        columns = []
        for i in range(j, blocks):
            columns.append(
                [
                    jnp.broadcast_to(rows[i][:, 8 * j + k : 8 * j + k + 1], (8, 128))
                    for k in range(8)
                ]
            )
        for k in range(8):
            lanes[8 * k : 8 * k + 8, :] = columns[0][k]
        a = [
            [jnp.broadcast_to(lanes[8 * k + m : 8 * k + m + 1, :], (8, 128)) for k in range(m + 1)]
            for m in range(8)
        ]
        right = [
            jnp.broadcast_to(aug[8 * j + k : 8 * j + k + 1, :], (8, 128)) for k in range(8)
        ]
        for k in range(8):
            root = lax.rsqrt(a[k][k])
            for m in range(k + 1, 8):
                a[m][k] = a[m][k] * root
            right[k] = right[k] * root
            for column in columns[1:]:
                column[k] = column[k] * root
            for m in range(k + 1, 8):
                for n in range(k + 1, m + 1):
                    a[m][n] = a[m][n] - a[m][k] * a[n][k]
                right[m] = right[m] - a[m][k] * right[k]
                for column in columns[1:]:
                    column[m] = column[m] - column[k] * a[m][k]
        for k in range(8):
            aug[8 * j + k : 8 * j + k + 1, :] = right[k][:1]
        for i in range(j + 1, blocks):
            column = columns[i - j]
            first = column[0] * right[0] + column[1] * right[1]
            second = column[2] * right[2] + column[3] * right[3]
            third = column[4] * right[4] + column[5] * right[5]
            fourth = column[6] * right[6] + column[7] * right[7]
            rows[i] = rows[i] - ((first + second) + (third + fourth))
    out_ref[...] = aug[...].T[rank : rank + cols, :] * scale


def whitened(terms, update_t, scale):
    cols, rank = update_t.shape
    return pl.pallas_call(
        functools.partial(whitened_kernel, scale),
        out_shape=jax.ShapeDtypeStruct((cols, rank), jnp.float32),
        in_specs=[ON_CHIP, ON_CHIP],
        out_specs=ON_CHIP,
        scratch_shapes=[pltpu.VMEM((rank, 2 * rank), jnp.float32)] * 2,
        compiler_params=pltpu.CompilerParams(vmem_limit_bytes=8 * 2**20),
        name="whitened",
    )(terms, update_t)


def per_device(tensor, y_factor, x_factor):
    width_x = x_factor.shape[1]
    kept, sent, folded_part = projected(tensor, y_factor, x_factor)
    folded, come = summed_everywhere(folded_part, sent)
    parts = update_parts(kept, come, folded, lax.axis_size("z"))
    update_t, wide = own_update(exchanged(parts, "z"))
    wide = with_neighbour(with_neighbour(wide, "core"), "z")
    total_x = width_x * lax.axis_size(GX)
    return whitened(of_everyone(wide, CHIPS), update_t, float(total_x) ** 0.5).T


def solution(mesh):
    finer = Mesh(mesh.devices.reshape(2, 4, 2, 2, 8), AXES)
    in_specs = (P(None, GX, GY), P(GY, None), P(None, GX))
    out_specs = P(None, AXES)
    return jax.shard_map(
        per_device, mesh=finer, in_specs=in_specs, out_specs=out_specs, check_vma=False
    )
```

```python
import functools

import jax
import jax.numpy as jnp
from jax import lax
from jax.experimental import pallas as pl
from jax.experimental.pallas import tpu as pltpu
from jax.sharding import Mesh
from jax.sharding import PartitionSpec as P


AXES = ("y_lo", "x", "core", "y_hi", "z")
GX = ("y_lo", "x", "core")
GY = ("y_hi", "z")
Y = ("y_lo", "y_hi")
CHIPS = ("y_hi", "y_lo", "x")
HIGHEST = lax.Precision.HIGHEST
EARLY = 6
CLASSES = 4
ON_CHIP = pl.BlockSpec(memory_space=pltpu.VMEM)


def exchanged(tiles, axis):
    return lax.all_to_all(tiles, axis, 0, 0, tiled=True)


def of_everyone(tile, axis):
    return exchanged(jnp.broadcast_to(tile[None], (lax.axis_size(axis), *tile.shape)), axis)


def tiles_of(matrix):
    rows, cols = matrix.shape
    return matrix.reshape(rows // 8, 8, cols // 128, 128).swapaxes(1, 2).reshape(-1, 8, 128)


def from_tiles(tiles, rows, cols):
    return tiles.reshape(rows // 8, cols // 128, 8, 128).swapaxes(1, 2).reshape(rows, cols)


def from_partner(array, axis):
    return lax.ppermute(array, axis, [(i, i ^ 1) for i in range(lax.axis_size(axis))])


def with_neighbour(value, axis):
    return value + from_partner(value, axis)


def ring_terms(value, axis):
    n = lax.axis_size(axis)
    at = [0, 2, 1, 3] if axis == Y else list(range(n))

    def shifted(by):
        return lax.ppermute(value, axis, [(at[i], at[(i + by) % n]) for i in range(n)])

    right, left, far = shifted(n - 1), shifted(1), shifted(2)
    return value, far, left, right


def with_ring(value, axis):
    own, far, left, right = ring_terms(value, axis)
    return (own + far) + (left + right)


def summed_everywhere(matrix, sent):
    rows, cols = matrix.shape
    tiles = tiles_of(with_neighbour(matrix, "core")).reshape(lax.axis_size(CHIPS), -1, 128)
    own = jnp.sum(exchanged(tiles, CHIPS), axis=0)
    come = from_partner(sent, "y_hi")
    own = jnp.sum(of_everyone(own, "z"), axis=0)
    return from_tiles(of_everyone(own, CHIPS).reshape(-1, 8, 128), rows, cols), come


def rounded_parts(matrix):
    high = matrix.astype(jnp.bfloat16)
    rest = matrix - high.astype(jnp.float32)
    middle = rest.astype(jnp.bfloat16)
    low = (rest - middle.astype(jnp.float32)).astype(jnp.bfloat16)
    return high, middle, low


def project_kernel(
    tensor_ref,
    y_ref,
    x_ref,
    kept_ref,
    sent_ref,
    folded_ref,
    planes,
    y_here,
    x_here,
    arrived,
):
    depth, width_x, _ = planes.shape
    rank = y_ref.shape[0]
    half = width_x // 2
    y_copy = pltpu.make_async_copy(y_ref, y_here, arrived.at[depth])
    x_copy = pltpu.make_async_copy(x_ref, x_here, arrived.at[depth + 1])
    y_copy.start()

    def plane(z):
        return pltpu.make_async_copy(tensor_ref.at[z], planes.at[z], arrived.at[z])

    for z in range(EARLY):
        plane(z).start()
    x_copy.start()
    kept_at = pl.multiple_of(lax.axis_index("y_hi") * half, half)
    sides = ((kept_ref, kept_at), (sent_ref, pl.multiple_of(half - kept_at, half)))
    y_copy.wait()
    y_t = y_here[...]
    none = jnp.zeros_like(y_t)
    y_left, y_right = jnp.concatenate([y_t, none], axis=0), jnp.concatenate([none, y_t], axis=0)
    contract = (((1,), (1,)), ((), ()))
    pairs = depth // 2
    for step in range(pairs + 1):
        if step < pairs:
            plane(2 * step).wait()
            plane(2 * step + 1).wait()
            for z in range(2 * step + EARLY, min(2 * step + EARLY + 2, depth)):
                plane(z).start()
        if step == 1:
            x_copy.wait()
        folded = None
        for there, start in sides:
            if step < pairs:
                rows = pl.ds(start, half)
                left = lax.dot_general(
                    planes[2 * step, rows, :], y_left, contract, preferred_element_type=jnp.float32
                )
                right = lax.dot_general(
                    planes[2 * step + 1, rows, :],
                    y_right,
                    contract,
                    preferred_element_type=jnp.float32,
                )
                there[:, pl.ds(2 * rank * step, 2 * rank)] = left + right
            if step > 0:
                x_part = x_here[:, pl.ds(start, half)]
                for part in rounded_parts(there[:, pl.ds(2 * rank * (step - 1), 2 * rank)]):
                    term = jnp.dot(x_part, part, preferred_element_type=jnp.float32)
                    folded = term if folded is None else folded + term
        if step > 0:
            folded_ref[:, pl.ds(2 * rank * (step - 1), 2 * rank)] = folded


def projected(tensor, y_factor, x_factor):
    depth, width_x, width_y = tensor.shape
    rank = y_factor.shape[1]
    rows = depth * rank
    return pl.pallas_call(
        project_kernel,
        out_shape=[
            jax.ShapeDtypeStruct((n, rows), jnp.float32)
            for n in (width_x // 2, width_x // 2, rank)
        ],
        in_specs=[pl.BlockSpec(memory_space=pltpu.HBM)] * 3,
        out_specs=[ON_CHIP] * 3,
        scratch_shapes=[
            pltpu.VMEM(tensor.shape, tensor.dtype),
            pltpu.VMEM((rank, width_y), y_factor.dtype),
            pltpu.VMEM(x_factor.shape, x_factor.dtype),
            pltpu.SemaphoreType.DMA((depth + 2,)),
        ],
        compiler_params=pltpu.CompilerParams(vmem_limit_bytes=24 * 2**20),
        name="projected",
    )(*(pltpu.with_memory_space_constraint(a, pltpu.HBM) for a in (tensor, y_factor.T, x_factor)))


def update_kernel(kept_ref, come_ref, folded_ref, out_ref):
    n, rows, lanes = out_ref.shape
    rank = lanes // 2
    half = kept_ref.shape[0] // n // 2
    part = lax.dot_general(
        kept_ref[...] + come_ref[...],
        folded_ref[...],
        (((1,), (1,)), ((), ())),
        precision=HIGHEST,
        preferred_element_type=jnp.float32,
    )
    part = part.reshape(n, 2, half, rank)
    packed = jnp.concatenate([part[:, 0], part[:, 1]], axis=2)
    classes = n * half // rows
    packed = packed.reshape(n // classes, classes, half, lanes)
    for z in range(n):
        out_ref[z] = packed[:, z % classes].reshape(rows, lanes)


def update_parts(kept, come, folded, n):
    width_x = kept.shape[0]
    rank = folded.shape[0]
    return pl.pallas_call(
        update_kernel,
        out_shape=jax.ShapeDtypeStruct((n, width_x // CLASSES // 2, 2 * rank), jnp.float32),
        in_specs=[ON_CHIP] * 3,
        out_specs=ON_CHIP,
        compiler_params=pltpu.CompilerParams(vmem_limit_bytes=24 * 2**20),
        name="update_parts",
    )(kept, come, folded)


def cross_kernel(parts_ref, update_ref, cross_ref, packed_ref):
    rank = update_ref.shape[1]
    half = update_ref.shape[0] // 2
    packed = jnp.sum(parts_ref[...], axis=0)
    packed_ref[...] = packed
    update_t = jnp.concatenate([packed[:, :rank], packed[:, rank:]], axis=0)
    square = lax.dot_general(
        update_t,
        update_t,
        (((0,), (0,)), ((), ())),
        precision=HIGHEST,
        preferred_element_type=jnp.float32,
    )
    cross_ref[...] = jnp.concatenate([square[: rank // 2], square[rank // 2 :]], axis=1)
    start = pl.multiple_of(lax.axis_index("z") // CLASSES * half, half)
    own = packed_ref[pl.ds(start, half), :]
    update_ref[...] = jnp.concatenate([own[:, :rank], own[:, rank:]], axis=0)


def own_update(parts):
    n, rows, lanes = parts.shape
    rank = lanes // 2
    return pl.pallas_call(
        cross_kernel,
        out_shape=(
            jax.ShapeDtypeStruct((2 * rows * CLASSES // n, rank), jnp.float32),
            jax.ShapeDtypeStruct((rank // 2, 2 * rank), jnp.float32),
        ),
        in_specs=[ON_CHIP],
        out_specs=(ON_CHIP, ON_CHIP),
        scratch_shapes=[pltpu.VMEM((rows, lanes), jnp.float32)],
        compiler_params=pltpu.CompilerParams(vmem_limit_bytes=8 * 2**20),
        name="own_update",
    )(parts)


def whitened_kernel(scale, own_ref, far_ref, left_ref, right_ref, update_ref, out_ref, aug, lanes):
    rank = update_ref.shape[1]
    cols = update_ref.shape[0]
    blocks = rank // 8
    wide = (own_ref[...] + far_ref[...]) + (left_ref[...] + right_ref[...])
    gram = jnp.concatenate([wide[:, :rank], wide[:, rank:]], axis=0)
    padded = jnp.concatenate(
        [update_ref[...], jnp.zeros((rank - cols, rank), jnp.float32)], axis=0
    )
    aug[...] = jnp.concatenate([gram, padded.T], axis=1)
    rows = [aug[8 * i : 8 * i + 8, :] for i in range(blocks)]
    for j in range(blocks):
        aug[8 * j : 8 * j + 8, :] = rows[j]
        columns = []
        for i in range(j, blocks):
            columns.append(
                [
                    jnp.broadcast_to(rows[i][:, 8 * j + k : 8 * j + k + 1], (8, 128))
                    for k in range(8)
                ]
            )
        for k in range(8):
            lanes[8 * k : 8 * k + 8, :] = columns[0][k]
        a = [
            [jnp.broadcast_to(lanes[8 * k + m : 8 * k + m + 1, :], (8, 128)) for k in range(m + 1)]
            for m in range(8)
        ]
        right = [
            jnp.broadcast_to(aug[8 * j + k : 8 * j + k + 1, :], (8, 128)) for k in range(8)
        ]
        for k in range(8):
            root = lax.rsqrt(a[k][k])
            for m in range(k + 1, 8):
                a[m][k] = a[m][k] * root
            right[k] = right[k] * root
            for column in columns[1:]:
                column[k] = column[k] * root
            for m in range(k + 1, 8):
                for n in range(k + 1, m + 1):
                    a[m][n] = a[m][n] - a[m][k] * a[n][k]
                right[m] = right[m] - a[m][k] * right[k]
                for column in columns[1:]:
                    column[m] = column[m] - column[k] * a[m][k]
        for k in range(8):
            aug[8 * j + k : 8 * j + k + 1, :] = right[k][:1]
        for i in range(j + 1, blocks):
            column = columns[i - j]
            first = column[0] * right[0] + column[1] * right[1]
            second = column[2] * right[2] + column[3] * right[3]
            third = column[4] * right[4] + column[5] * right[5]
            fourth = column[6] * right[6] + column[7] * right[7]
            rows[i] = rows[i] - ((first + second) + (third + fourth))
    out_ref[...] = aug[...].T[rank : rank + cols, :] * scale


def whitened(terms, update_t, scale):
    cols, rank = update_t.shape
    return pl.pallas_call(
        functools.partial(whitened_kernel, scale),
        out_shape=jax.ShapeDtypeStruct((cols, rank), jnp.float32),
        in_specs=[ON_CHIP] * 5,
        out_specs=ON_CHIP,
        scratch_shapes=[pltpu.VMEM((rank, 2 * rank), jnp.float32)] * 2,
        compiler_params=pltpu.CompilerParams(vmem_limit_bytes=8 * 2**20),
        name="whitened",
    )(*terms, update_t)


def new_basis(tensor, y_factor, x_factor):
    width_x = x_factor.shape[1]
    kept, sent, folded_part = projected(tensor, y_factor, x_factor)
    folded, come = summed_everywhere(folded_part, sent)
    parts = update_parts(kept, come, folded, lax.axis_size("z"))
    update_t, wide = own_update(exchanged(parts, "z"))
    wide = with_ring(with_ring(with_neighbour(wide, "core"), "z"), "x")
    total_x = width_x * lax.axis_size(GX)
    return whitened(ring_terms(wide, Y), update_t, float(total_x) ** 0.5).T


def solution(mesh):
    finer = Mesh(mesh.devices.reshape(2, 4, 2, 2, 8), AXES)
    in_specs = (P(None, GX, GY), P(GY, None), P(None, GX))
    out_specs = P(None, AXES)
    return jax.shard_map(
        new_basis, mesh=finer, in_specs=in_specs, out_specs=out_specs, check_vma=False
    )
```

```python
import functools

import jax
import jax.numpy as jnp
from jax import lax
from jax.experimental import pallas as pl
from jax.experimental.pallas import tpu as pltpu
from jax.sharding import Mesh
from jax.sharding import PartitionSpec as P


AXES = ("y_lo", "x", "core", "y_hi", "z")
GX = ("y_lo", "x", "core")
GY = ("y_hi", "z")
CHIPS = ("y_hi", "y_lo", "x")
NEAR = ("y_lo", "x")
HIGHEST = lax.Precision.HIGHEST
EARLY = 6
ON_CHIP = pl.BlockSpec(memory_space=pltpu.VMEM)


def exchanged(tiles, axis):
    return lax.all_to_all(tiles, axis, 0, 0, tiled=True)


def of_everyone(tile, axis):
    return exchanged(jnp.broadcast_to(tile[None], (lax.axis_size(axis), *tile.shape)), axis)


def tiles_of(matrix):
    rows, cols = matrix.shape
    return matrix.reshape(rows // 8, 8, cols // 128, 128).swapaxes(1, 2).reshape(-1, 8, 128)


def from_tiles(tiles, rows, cols):
    return tiles.reshape(rows // 8, cols // 128, 8, 128).swapaxes(1, 2).reshape(rows, cols)


def from_partner(array, axis):
    return lax.ppermute(array, axis, [(i, i ^ 1) for i in range(lax.axis_size(axis))])


def with_neighbour(value, axis):
    return value + from_partner(value, axis)


def summed_everywhere(matrix, sent):
    rows, cols = matrix.shape
    tiles = tiles_of(with_neighbour(matrix, "core")).reshape(lax.axis_size(NEAR), -1, 128)
    tiles = jnp.broadcast_to(tiles[None], (lax.axis_size("y_hi"), *tiles.shape))
    tiles = tiles.reshape(lax.axis_size(CHIPS), -1, 128)
    own = jnp.sum(exchanged(tiles, CHIPS), axis=0)
    come = from_partner(sent, "y_hi")
    own = jnp.sum(of_everyone(own, "z"), axis=0)
    own, come = lax.optimization_barrier((own, come))
    return from_tiles(of_everyone(own, NEAR).reshape(-1, 8, 128), rows, cols), come


def rounded_parts(matrix):
    high = matrix.astype(jnp.bfloat16)
    rest = matrix - high.astype(jnp.float32)
    middle = rest.astype(jnp.bfloat16)
    low = (rest - middle.astype(jnp.float32)).astype(jnp.bfloat16)
    return high, middle, low


def project_kernel(
    tensor_ref,
    y_ref,
    x_ref,
    kept_ref,
    sent_ref,
    folded_ref,
    planes,
    y_here,
    x_here,
    arrived,
):
    depth, width_x, _ = planes.shape
    rank = y_ref.shape[0]
    half = width_x // 2
    y_copy = pltpu.make_async_copy(y_ref, y_here, arrived.at[depth])
    x_copy = pltpu.make_async_copy(x_ref, x_here, arrived.at[depth + 1])
    y_copy.start()

    def plane(z):
        return pltpu.make_async_copy(tensor_ref.at[z], planes.at[z], arrived.at[z])

    for z in range(EARLY):
        plane(z).start()
    x_copy.start()
    kept_at = pl.multiple_of(lax.axis_index("y_hi") * half, half)
    sides = ((kept_ref, kept_at), (sent_ref, pl.multiple_of(half - kept_at, half)))
    y_copy.wait()
    y_t = y_here[...]
    none = jnp.zeros_like(y_t)
    y_left, y_right = jnp.concatenate([y_t, none], axis=0), jnp.concatenate([none, y_t], axis=0)
    contract = (((1,), (1,)), ((), ()))
    pairs = depth // 2
    for step in range(pairs + 1):
        if step < pairs:
            plane(2 * step).wait()
            plane(2 * step + 1).wait()
            for z in range(2 * step + EARLY, min(2 * step + EARLY + 2, depth)):
                plane(z).start()
        if step == 1:
            x_copy.wait()
        folded = None
        for there, start in sides:
            if step < pairs:
                rows = pl.ds(start, half)
                left = lax.dot_general(
                    planes[2 * step, rows, :], y_left, contract, preferred_element_type=jnp.float32
                )
                right = lax.dot_general(
                    planes[2 * step + 1, rows, :],
                    y_right,
                    contract,
                    preferred_element_type=jnp.float32,
                )
                there[:, pl.ds(2 * rank * step, 2 * rank)] = left + right
            if step > 0:
                x_part = x_here[:, pl.ds(start, half)]
                for part in rounded_parts(there[:, pl.ds(2 * rank * (step - 1), 2 * rank)]):
                    term = jnp.dot(x_part, part, preferred_element_type=jnp.float32)
                    folded = term if folded is None else folded + term
        if step > 0:
            folded_ref[:, pl.ds(2 * rank * (step - 1), 2 * rank)] = folded


def projected(tensor, y_factor, x_factor):
    depth, width_x, width_y = tensor.shape
    rank = y_factor.shape[1]
    rows = depth * rank
    return pl.pallas_call(
        project_kernel,
        out_shape=[
            jax.ShapeDtypeStruct((n, rows), jnp.float32)
            for n in (width_x // 2, width_x // 2, rank)
        ],
        in_specs=[pl.BlockSpec(memory_space=pltpu.HBM)] * 3,
        out_specs=[ON_CHIP] * 3,
        scratch_shapes=[
            pltpu.VMEM(tensor.shape, tensor.dtype),
            pltpu.VMEM((rank, width_y), y_factor.dtype),
            pltpu.VMEM(x_factor.shape, x_factor.dtype),
            pltpu.SemaphoreType.DMA((depth + 2,)),
        ],
        compiler_params=pltpu.CompilerParams(vmem_limit_bytes=24 * 2**20),
        name="projected",
    )(*(pltpu.with_memory_space_constraint(a, pltpu.HBM) for a in (tensor, y_factor.T, x_factor)))


def update_kernel(kept_ref, come_ref, folded_ref, out_ref):
    n, rows, lanes = out_ref.shape
    rank = lanes // 2
    half = 2 * rows // n
    part = lax.dot_general(
        kept_ref[...] + come_ref[...],
        folded_ref[...],
        (((1,), (1,)), ((), ())),
        precision=HIGHEST,
        preferred_element_type=jnp.float32,
    )
    part = part.reshape(n, 2, half, rank)
    packed = jnp.concatenate([part[:, 0], part[:, 1]], axis=2)
    packed = packed.reshape(n // 2, 2, half, lanes)
    for z in range(n):
        out_ref[z] = packed[:, z % 2].reshape(rows, lanes)


def update_parts(kept, come, folded, n):
    width_x = kept.shape[0]
    rank = folded.shape[0]
    return pl.pallas_call(
        update_kernel,
        out_shape=jax.ShapeDtypeStruct((n, width_x // 4, 2 * rank), jnp.float32),
        in_specs=[ON_CHIP] * 3,
        out_specs=ON_CHIP,
        compiler_params=pltpu.CompilerParams(vmem_limit_bytes=24 * 2**20),
        name="update_parts",
    )(kept, come, folded)


def cross_kernel(parts_ref, update_ref, cross_ref, packed_ref):
    rank = update_ref.shape[1]
    half = update_ref.shape[0] // 2
    packed = jnp.sum(parts_ref[...], axis=0)
    packed_ref[...] = packed
    update_t = jnp.concatenate([packed[:, :rank], packed[:, rank:]], axis=0)
    square = lax.dot_general(
        update_t,
        update_t,
        (((0,), (0,)), ((), ())),
        precision=HIGHEST,
        preferred_element_type=jnp.float32,
    )
    cross_ref[...] = jnp.concatenate([square[: rank // 2], square[rank // 2 :]], axis=1)
    start = pl.multiple_of(lax.axis_index("z") // 2 * half, half)
    own = packed_ref[pl.ds(start, half), :]
    update_ref[...] = jnp.concatenate([own[:, :rank], own[:, rank:]], axis=0)


def own_update(parts):
    n, rows, lanes = parts.shape
    rank = lanes // 2
    return pl.pallas_call(
        cross_kernel,
        out_shape=(
            jax.ShapeDtypeStruct((4 * rows // n, rank), jnp.float32),
            jax.ShapeDtypeStruct((rank // 2, 2 * rank), jnp.float32),
        ),
        in_specs=[ON_CHIP],
        out_specs=(ON_CHIP, ON_CHIP),
        scratch_shapes=[pltpu.VMEM((rows, lanes), jnp.float32)],
        compiler_params=pltpu.CompilerParams(vmem_limit_bytes=8 * 2**20),
        name="own_update",
    )(parts)


def whitened_kernel(scale, cross_ref, update_ref, out_ref, aug, lanes):
    rank = update_ref.shape[1]
    cols = update_ref.shape[0]
    blocks = rank // 8
    wide = cross_ref[0]
    for i in range(1, cross_ref.shape[0]):
        wide = wide + cross_ref[i]
    gram = jnp.concatenate([wide[:, :rank], wide[:, rank:]], axis=0)
    padded = jnp.concatenate(
        [update_ref[...], jnp.zeros((rank - cols, rank), jnp.float32)], axis=0
    )
    aug[...] = jnp.concatenate([gram, padded.T], axis=1)
    rows = [aug[8 * i : 8 * i + 8, :] for i in range(blocks)]
    for j in range(blocks):
        aug[8 * j : 8 * j + 8, :] = rows[j]
        columns = []
        for i in range(j, blocks):
            columns.append(
                [
                    jnp.broadcast_to(rows[i][:, 8 * j + k : 8 * j + k + 1], (8, 128))
                    for k in range(8)
                ]
            )
        for k in range(8):
            lanes[8 * k : 8 * k + 8, :] = columns[0][k]
        a = [
            [jnp.broadcast_to(lanes[8 * k + m : 8 * k + m + 1, :], (8, 128)) for k in range(m + 1)]
            for m in range(8)
        ]
        right = [
            jnp.broadcast_to(aug[8 * j + k : 8 * j + k + 1, :], (8, 128)) for k in range(8)
        ]
        for k in range(8):
            root = lax.rsqrt(a[k][k])
            for m in range(k + 1, 8):
                a[m][k] = a[m][k] * root
            right[k] = right[k] * root
            for column in columns[1:]:
                column[k] = column[k] * root
            for m in range(k + 1, 8):
                for n in range(k + 1, m + 1):
                    a[m][n] = a[m][n] - a[m][k] * a[n][k]
                right[m] = right[m] - a[m][k] * right[k]
                for column in columns[1:]:
                    column[m] = column[m] - column[k] * a[m][k]
        for k in range(8):
            aug[8 * j + k : 8 * j + k + 1, :] = right[k][:1]
        for i in range(j + 1, blocks):
            column = columns[i - j]
            first = column[0] * right[0] + column[1] * right[1]
            second = column[2] * right[2] + column[3] * right[3]
            third = column[4] * right[4] + column[5] * right[5]
            fourth = column[6] * right[6] + column[7] * right[7]
            rows[i] = rows[i] - ((first + second) + (third + fourth))
    out_ref[...] = aug[...].T[rank : rank + cols, :] * scale


def whitened(terms, update_t, scale):
    cols, rank = update_t.shape
    return pl.pallas_call(
        functools.partial(whitened_kernel, scale),
        out_shape=jax.ShapeDtypeStruct((cols, rank), jnp.float32),
        in_specs=[ON_CHIP, ON_CHIP],
        out_specs=ON_CHIP,
        scratch_shapes=[pltpu.VMEM((rank, 2 * rank), jnp.float32)] * 2,
        compiler_params=pltpu.CompilerParams(vmem_limit_bytes=8 * 2**20),
        name="whitened",
    )(terms, update_t)


def new_basis(tensor, y_factor, x_factor):
    width_x = x_factor.shape[1]
    kept, sent, folded_part = projected(tensor, y_factor, x_factor)
    folded, come = summed_everywhere(folded_part, sent)
    parts = update_parts(kept, come, folded, lax.axis_size("z"))
    update_t, wide = own_update(exchanged(parts, "z"))
    wide = with_neighbour(with_neighbour(wide, "core"), "z")
    total_x = width_x * lax.axis_size(GX)
    return whitened(of_everyone(wide, CHIPS), update_t, float(total_x) ** 0.5).T


def solution(mesh):
    finer = Mesh(mesh.devices.reshape(2, 4, 2, 2, 8), AXES)
    in_specs = (P(None, GX, GY), P(GY, None), P(None, GX))
    out_specs = P(None, AXES)
    return jax.shard_map(
        new_basis, mesh=finer, in_specs=in_specs, out_specs=out_specs, check_vma=False
    )
```

```python
import functools

import jax
import jax.numpy as jnp
from jax import lax
from jax.experimental import pallas as pl
from jax.experimental.pallas import tpu as pltpu
from jax.sharding import Mesh
from jax.sharding import PartitionSpec as P


AXES = ("y_lo", "x", "core", "y_hi", "z")
GX = ("y_lo", "x", "core")
GY = ("y_hi", "z")
CHIPS = ("y_hi", "y_lo", "x")
HIGHEST = lax.Precision.HIGHEST
EARLY = 6
ON_CHIP = pl.BlockSpec(memory_space=pltpu.VMEM)


def exchanged(tiles, axis):
    return lax.all_to_all(tiles, axis, 0, 0, tiled=True)


def of_everyone(tile, axis):
    return exchanged(jnp.broadcast_to(tile[None], (lax.axis_size(axis), *tile.shape)), axis)


def tiles_of(matrix):
    rows, cols = matrix.shape
    return matrix.reshape(rows // 8, 8, cols // 128, 128).swapaxes(1, 2).reshape(-1, 8, 128)


def from_tiles(tiles, rows, cols):
    return tiles.reshape(rows // 8, cols // 128, 8, 128).swapaxes(1, 2).reshape(rows, cols)


def from_partner(array, axis):
    return lax.ppermute(array, axis, [(i, i ^ 1) for i in range(lax.axis_size(axis))])


def with_neighbour(value, axis):
    return value + from_partner(value, axis)


def summed_everywhere(matrix, sent):
    rows, cols = matrix.shape
    tiles = tiles_of(matrix).reshape(lax.axis_size("z"), -1, 128)
    come = from_partner(sent, "y_hi")
    own = jnp.sum(exchanged(tiles, "z"), axis=0)
    own = jnp.sum(of_everyone(with_neighbour(own, "core"), CHIPS), axis=0)
    own, come = lax.optimization_barrier((own, come))
    return from_tiles(of_everyone(own, "z").reshape(-1, 8, 128), rows, cols), come


def rounded_parts(matrix):
    high = matrix.astype(jnp.bfloat16)
    rest = matrix - high.astype(jnp.float32)
    middle = rest.astype(jnp.bfloat16)
    low = (rest - middle.astype(jnp.float32)).astype(jnp.bfloat16)
    return high, middle, low


def project_kernel(
    tensor_ref,
    y_ref,
    x_ref,
    kept_ref,
    sent_ref,
    folded_ref,
    planes,
    y_here,
    x_here,
    arrived,
):
    depth, width_x, _ = planes.shape
    rank = y_ref.shape[0]
    half = width_x // 2
    y_copy = pltpu.make_async_copy(y_ref, y_here, arrived.at[depth])
    x_copy = pltpu.make_async_copy(x_ref, x_here, arrived.at[depth + 1])
    y_copy.start()

    def plane(z):
        return pltpu.make_async_copy(tensor_ref.at[z], planes.at[z], arrived.at[z])

    for z in range(EARLY):
        plane(z).start()
    x_copy.start()
    kept_at = pl.multiple_of(lax.axis_index("y_hi") * half, half)
    sides = ((kept_ref, kept_at), (sent_ref, pl.multiple_of(half - kept_at, half)))
    y_copy.wait()
    y_t = y_here[...]
    none = jnp.zeros_like(y_t)
    y_left, y_right = jnp.concatenate([y_t, none], axis=0), jnp.concatenate([none, y_t], axis=0)
    contract = (((1,), (1,)), ((), ()))
    pairs = depth // 2
    for step in range(pairs + 1):
        if step < pairs:
            plane(2 * step).wait()
            plane(2 * step + 1).wait()
            for z in range(2 * step + EARLY, min(2 * step + EARLY + 2, depth)):
                plane(z).start()
        if step == 1:
            x_copy.wait()
        folded = None
        for there, start in sides:
            if step < pairs:
                rows = pl.ds(start, half)
                left = lax.dot_general(
                    planes[2 * step, rows, :], y_left, contract, preferred_element_type=jnp.float32
                )
                right = lax.dot_general(
                    planes[2 * step + 1, rows, :],
                    y_right,
                    contract,
                    preferred_element_type=jnp.float32,
                )
                there[:, pl.ds(2 * rank * step, 2 * rank)] = left + right
            if step > 0:
                x_part = x_here[:, pl.ds(start, half)]
                for part in rounded_parts(there[:, pl.ds(2 * rank * (step - 1), 2 * rank)]):
                    term = jnp.dot(x_part, part, preferred_element_type=jnp.float32)
                    folded = term if folded is None else folded + term
        if step > 0:
            folded_ref[:, pl.ds(2 * rank * (step - 1), 2 * rank)] = folded


def projected(tensor, y_factor, x_factor):
    depth, width_x, width_y = tensor.shape
    rank = y_factor.shape[1]
    rows = depth * rank
    return pl.pallas_call(
        project_kernel,
        out_shape=[
            jax.ShapeDtypeStruct((n, rows), jnp.float32)
            for n in (width_x // 2, width_x // 2, rank)
        ],
        in_specs=[pl.BlockSpec(memory_space=pltpu.HBM)] * 3,
        out_specs=[ON_CHIP] * 3,
        scratch_shapes=[
            pltpu.VMEM(tensor.shape, tensor.dtype),
            pltpu.VMEM((rank, width_y), y_factor.dtype),
            pltpu.VMEM(x_factor.shape, x_factor.dtype),
            pltpu.SemaphoreType.DMA((depth + 2,)),
        ],
        compiler_params=pltpu.CompilerParams(vmem_limit_bytes=24 * 2**20),
        name="projected",
    )(*(pltpu.with_memory_space_constraint(a, pltpu.HBM) for a in (tensor, y_factor.T, x_factor)))


def update_kernel(kept_ref, come_ref, folded_ref, out_ref):
    n, rows, lanes = out_ref.shape
    rank = lanes // 2
    half = 2 * rows // n
    part = lax.dot_general(
        kept_ref[...] + come_ref[...],
        folded_ref[...],
        (((1,), (1,)), ((), ())),
        precision=HIGHEST,
        preferred_element_type=jnp.float32,
    )
    part = part.reshape(n, 2, half, rank)
    packed = jnp.concatenate([part[:, 0], part[:, 1]], axis=2)
    packed = packed.reshape(n // 2, 2, half, lanes)
    for z in range(n):
        out_ref[z] = packed[:, z % 2].reshape(rows, lanes)


def update_parts(kept, come, folded, n):
    width_x = kept.shape[0]
    rank = folded.shape[0]
    return pl.pallas_call(
        update_kernel,
        out_shape=jax.ShapeDtypeStruct((n, width_x // 4, 2 * rank), jnp.float32),
        in_specs=[ON_CHIP] * 3,
        out_specs=ON_CHIP,
        compiler_params=pltpu.CompilerParams(vmem_limit_bytes=24 * 2**20),
        name="update_parts",
    )(kept, come, folded)


def cross_kernel(parts_ref, update_ref, cross_ref, packed_ref):
    rank = update_ref.shape[1]
    half = update_ref.shape[0] // 2
    packed = jnp.sum(parts_ref[...], axis=0)
    packed_ref[...] = packed
    update_t = jnp.concatenate([packed[:, :rank], packed[:, rank:]], axis=0)
    square = lax.dot_general(
        update_t,
        update_t,
        (((0,), (0,)), ((), ())),
        precision=HIGHEST,
        preferred_element_type=jnp.float32,
    )
    cross_ref[...] = jnp.concatenate([square[: rank // 2], square[rank // 2 :]], axis=1)
    start = pl.multiple_of(lax.axis_index("z") // 2 * half, half)
    own = packed_ref[pl.ds(start, half), :]
    update_ref[...] = jnp.concatenate([own[:, :rank], own[:, rank:]], axis=0)


def own_update(parts):
    n, rows, lanes = parts.shape
    rank = lanes // 2
    return pl.pallas_call(
        cross_kernel,
        out_shape=(
            jax.ShapeDtypeStruct((4 * rows // n, rank), jnp.float32),
            jax.ShapeDtypeStruct((rank // 2, 2 * rank), jnp.float32),
        ),
        in_specs=[ON_CHIP],
        out_specs=(ON_CHIP, ON_CHIP),
        scratch_shapes=[pltpu.VMEM((rows, lanes), jnp.float32)],
        compiler_params=pltpu.CompilerParams(vmem_limit_bytes=8 * 2**20),
        name="own_update",
    )(parts)


def whitened_kernel(scale, cross_ref, update_ref, out_ref, aug, lanes):
    rank = update_ref.shape[1]
    cols = update_ref.shape[0]
    blocks = rank // 8
    wide = cross_ref[0]
    for i in range(1, cross_ref.shape[0]):
        wide = wide + cross_ref[i]
    gram = jnp.concatenate([wide[:, :rank], wide[:, rank:]], axis=0)
    padded = jnp.concatenate(
        [update_ref[...], jnp.zeros((rank - cols, rank), jnp.float32)], axis=0
    )
    aug[...] = jnp.concatenate([gram, padded.T], axis=1)
    rows = [aug[8 * i : 8 * i + 8, :] for i in range(blocks)]
    for j in range(blocks):
        aug[8 * j : 8 * j + 8, :] = rows[j]
        columns = []
        for i in range(j, blocks):
            columns.append(
                [
                    jnp.broadcast_to(rows[i][:, 8 * j + k : 8 * j + k + 1], (8, 128))
                    for k in range(8)
                ]
            )
        for k in range(8):
            lanes[8 * k : 8 * k + 8, :] = columns[0][k]
        a = [
            [jnp.broadcast_to(lanes[8 * k + m : 8 * k + m + 1, :], (8, 128)) for k in range(m + 1)]
            for m in range(8)
        ]
        right = [
            jnp.broadcast_to(aug[8 * j + k : 8 * j + k + 1, :], (8, 128)) for k in range(8)
        ]
        for k in range(8):
            root = lax.rsqrt(a[k][k])
            for m in range(k + 1, 8):
                a[m][k] = a[m][k] * root
            right[k] = right[k] * root
            for column in columns[1:]:
                column[k] = column[k] * root
            for m in range(k + 1, 8):
                for n in range(k + 1, m + 1):
                    a[m][n] = a[m][n] - a[m][k] * a[n][k]
                right[m] = right[m] - a[m][k] * right[k]
                for column in columns[1:]:
                    column[m] = column[m] - column[k] * a[m][k]
        for k in range(8):
            aug[8 * j + k : 8 * j + k + 1, :] = right[k][:1]
        for i in range(j + 1, blocks):
            column = columns[i - j]
            first = column[0] * right[0] + column[1] * right[1]
            second = column[2] * right[2] + column[3] * right[3]
            third = column[4] * right[4] + column[5] * right[5]
            fourth = column[6] * right[6] + column[7] * right[7]
            rows[i] = rows[i] - ((first + second) + (third + fourth))
    out_ref[...] = aug[...].T[rank : rank + cols, :] * scale


def whitened(terms, update_t, scale):
    cols, rank = update_t.shape
    return pl.pallas_call(
        functools.partial(whitened_kernel, scale),
        out_shape=jax.ShapeDtypeStruct((cols, rank), jnp.float32),
        in_specs=[ON_CHIP, ON_CHIP],
        out_specs=ON_CHIP,
        scratch_shapes=[pltpu.VMEM((rank, 2 * rank), jnp.float32)] * 2,
        compiler_params=pltpu.CompilerParams(vmem_limit_bytes=8 * 2**20),
        name="whitened",
    )(terms, update_t)


def new_basis(tensor, y_factor, x_factor):
    width_x = x_factor.shape[1]
    kept, sent, folded_part = projected(tensor, y_factor, x_factor)
    folded, come = summed_everywhere(folded_part, sent)
    parts = update_parts(kept, come, folded, lax.axis_size("z"))
    update_t, wide = own_update(exchanged(parts, "z"))
    wide = with_neighbour(with_neighbour(wide, "core"), "z")
    total_x = width_x * lax.axis_size(GX)
    return whitened(of_everyone(wide, CHIPS), update_t, float(total_x) ** 0.5).T


def solution(mesh):
    finer = Mesh(mesh.devices.reshape(2, 4, 2, 2, 8), AXES)
    in_specs = (P(None, GX, GY), P(GY, None), P(None, GX))
    out_specs = P(None, AXES)
    return jax.shard_map(
        new_basis, mesh=finer, in_specs=in_specs, out_specs=out_specs, check_vma=False
    )
```

```python
import functools

import jax
import jax.numpy as jnp
from jax import lax
from jax.experimental import pallas as pl
from jax.experimental.pallas import tpu as pltpu
from jax.sharding import Mesh
from jax.sharding import PartitionSpec as P

AXES = ("y_lo", "x", "core", "y_hi", "z")
GX = ("y_lo", "x", "core")
GY = ("y_hi", "z")
CHIPS = ("y_hi", "y_lo", "x")
NEAR = ("y_lo", "x")
HIGHEST = lax.Precision.HIGHEST
EARLY = 6
ON_CHIP = pl.BlockSpec(memory_space=pltpu.VMEM)


def exchanged(tiles, axis):
    return lax.all_to_all(tiles, axis, 0, 0, tiled=True)


def of_everyone(tile, axis):
    return exchanged(jnp.broadcast_to(tile[None], (lax.axis_size(axis), *tile.shape)), axis)


def tiles_of(matrix):
    rows, cols = matrix.shape
    return matrix.reshape(rows // 8, 8, cols // 128, 128).swapaxes(1, 2).reshape(-1, 8, 128)


def from_tiles(tiles, rows, cols):
    return tiles.reshape(rows // 8, cols // 128, 8, 128).swapaxes(1, 2).reshape(rows, cols)


def from_partner(array, axis):
    return lax.ppermute(array, axis, [(i, i ^ 1) for i in range(lax.axis_size(axis))])


def with_neighbour(value, axis):
    return value + from_partner(value, axis)


def summed_everywhere(matrix, sent):
    rows, cols = matrix.shape
    tiles = tiles_of(with_neighbour(matrix, "core")).reshape(lax.axis_size(NEAR), -1, 128)
    tiles = jnp.broadcast_to(tiles[None], (lax.axis_size("y_hi"), *tiles.shape))
    tiles = tiles.reshape(lax.axis_size(CHIPS), -1, 128)
    own = jnp.sum(exchanged(tiles, CHIPS), axis=0)
    own, sent = lax.optimization_barrier((own, sent))
    come = from_partner(sent, "y_hi")
    own = jnp.sum(of_everyone(own, "z"), axis=0)
    own, come = lax.optimization_barrier((own, come))
    return from_tiles(of_everyone(own, NEAR).reshape(-1, 8, 128), rows, cols), come


def rounded_parts(matrix):
    high = matrix.astype(jnp.bfloat16)
    rest = matrix - high.astype(jnp.float32)
    middle = rest.astype(jnp.bfloat16)
    low = (rest - middle.astype(jnp.float32)).astype(jnp.bfloat16)
    return high, middle, low


def project_kernel(
    tensor_ref,
    y_ref,
    x_ref,
    kept_ref,
    sent_ref,
    folded_ref,
    planes,
    y_here,
    x_here,
    arrived,
):
    depth, width_x, _ = planes.shape
    rank = y_ref.shape[0]
    half = width_x // 2
    y_copy = pltpu.make_async_copy(y_ref, y_here, arrived.at[depth])
    x_copy = pltpu.make_async_copy(x_ref, x_here, arrived.at[depth + 1])
    y_copy.start()

    def plane(z):
        return pltpu.make_async_copy(tensor_ref.at[z], planes.at[z], arrived.at[z])

    for z in range(EARLY):
        plane(z).start()
    x_copy.start()
    kept_at = pl.multiple_of(lax.axis_index("y_hi") * half, half)
    sides = ((kept_ref, kept_at), (sent_ref, pl.multiple_of(half - kept_at, half)))
    y_copy.wait()
    y_t = y_here[...]
    none = jnp.zeros_like(y_t)
    y_left, y_right = jnp.concatenate([y_t, none], axis=0), jnp.concatenate([none, y_t], axis=0)
    contract = (((1,), (1,)), ((), ()))
    pairs = depth // 2
    for step in range(pairs + 1):
        if step < pairs:
            plane(2 * step).wait()
            plane(2 * step + 1).wait()
            for z in range(2 * step + EARLY, min(2 * step + EARLY + 2, depth)):
                plane(z).start()
        if step == 1:
            x_copy.wait()
        folded = None
        for there, start in sides:
            if step < pairs:
                rows = pl.ds(start, half)
                left = lax.dot_general(
                    planes[2 * step, rows, :], y_left, contract, preferred_element_type=jnp.float32
                )
                right = lax.dot_general(
                    planes[2 * step + 1, rows, :],
                    y_right,
                    contract,
                    preferred_element_type=jnp.float32,
                )
                there[:, pl.ds(2 * rank * step, 2 * rank)] = left + right
            if step > 0:
                x_part = x_here[:, pl.ds(start, half)]
                for part in rounded_parts(there[:, pl.ds(2 * rank * (step - 1), 2 * rank)]):
                    term = jnp.dot(x_part, part, preferred_element_type=jnp.float32)
                    folded = term if folded is None else folded + term
        if step > 0:
            folded_ref[:, pl.ds(2 * rank * (step - 1), 2 * rank)] = folded


def projected(tensor, y_factor, x_factor):
    depth, width_x, width_y = tensor.shape
    rank = y_factor.shape[1]
    rows = depth * rank
    return pl.pallas_call(
        project_kernel,
        out_shape=[
            jax.ShapeDtypeStruct((n, rows), jnp.float32)
            for n in (width_x // 2, width_x // 2, rank)
        ],
        in_specs=[pl.BlockSpec(memory_space=pltpu.HBM)] * 3,
        out_specs=[ON_CHIP] * 3,
        scratch_shapes=[
            pltpu.VMEM(tensor.shape, tensor.dtype),
            pltpu.VMEM((rank, width_y), y_factor.dtype),
            pltpu.VMEM(x_factor.shape, x_factor.dtype),
            pltpu.SemaphoreType.DMA((depth + 2,)),
        ],
        compiler_params=pltpu.CompilerParams(vmem_limit_bytes=24 * 2**20),
        name="projected",
    )(*(pltpu.with_memory_space_constraint(a, pltpu.HBM) for a in (tensor, y_factor.T, x_factor)))


def update_kernel(kept_ref, come_ref, folded_ref, out_ref):
    n, rows, lanes = out_ref.shape
    rank = lanes // 2
    half = 2 * rows // n
    part = lax.dot_general(
        kept_ref[...] + come_ref[...],
        folded_ref[...],
        (((1,), (1,)), ((), ())),
        precision=HIGHEST,
        preferred_element_type=jnp.float32,
    )
    part = part.reshape(n, 2, half, rank)
    packed = jnp.concatenate([part[:, 0], part[:, 1]], axis=2)
    packed = packed.reshape(n // 2, 2, half, lanes)
    for z in range(n):
        out_ref[z] = packed[:, z % 2].reshape(rows, lanes)


def update_parts(kept, come, folded, n):
    width_x = kept.shape[0]
    rank = folded.shape[0]
    return pl.pallas_call(
        update_kernel,
        out_shape=jax.ShapeDtypeStruct((n, width_x // 4, 2 * rank), jnp.float32),
        in_specs=[ON_CHIP] * 3,
        out_specs=ON_CHIP,
        compiler_params=pltpu.CompilerParams(vmem_limit_bytes=24 * 2**20),
        name="update_parts",
    )(kept, come, folded)


def cross_kernel(parts_ref, update_ref, cross_ref, packed_ref):
    rank = update_ref.shape[1]
    half = update_ref.shape[0] // 2
    packed = jnp.sum(parts_ref[...], axis=0)
    packed_ref[...] = packed
    update_t = jnp.concatenate([packed[:, :rank], packed[:, rank:]], axis=0)
    square = lax.dot_general(
        update_t,
        update_t,
        (((0,), (0,)), ((), ())),
        precision=HIGHEST,
        preferred_element_type=jnp.float32,
    )
    cross_ref[...] = jnp.concatenate([square[: rank // 2], square[rank // 2 :]], axis=1)
    start = pl.multiple_of(lax.axis_index("z") // 2 * half, half)
    own = packed_ref[pl.ds(start, half), :]
    update_ref[...] = jnp.concatenate([own[:, :rank], own[:, rank:]], axis=0)


def own_update(parts):
    n, rows, lanes = parts.shape
    rank = lanes // 2
    return pl.pallas_call(
        cross_kernel,
        out_shape=(
            jax.ShapeDtypeStruct((4 * rows // n, rank), jnp.float32),
            jax.ShapeDtypeStruct((rank // 2, 2 * rank), jnp.float32),
        ),
        in_specs=[ON_CHIP],
        out_specs=(ON_CHIP, ON_CHIP),
        scratch_shapes=[pltpu.VMEM((rows, lanes), jnp.float32)],
        compiler_params=pltpu.CompilerParams(vmem_limit_bytes=8 * 2**20),
        name="own_update",
    )(parts)


def whitened_kernel(scale, cross_ref, update_ref, out_ref, aug, lanes):
    rank = update_ref.shape[1]
    cols = update_ref.shape[0]
    blocks = rank // 8
    wide = cross_ref[0]
    for i in range(1, cross_ref.shape[0]):
        wide = wide + cross_ref[i]
    gram = jnp.concatenate([wide[:, :rank], wide[:, rank:]], axis=0)
    padded = jnp.concatenate(
        [update_ref[...], jnp.zeros((rank - cols, rank), jnp.float32)], axis=0
    )
    aug[...] = jnp.concatenate([gram, padded.T], axis=1)
    rows = [aug[8 * i : 8 * i + 8, :] for i in range(blocks)]
    for j in range(blocks):
        aug[8 * j : 8 * j + 8, :] = rows[j]
        columns = []
        for i in range(j, blocks):
            columns.append(
                [
                    jnp.broadcast_to(rows[i][:, 8 * j + k : 8 * j + k + 1], (8, 128))
                    for k in range(8)
                ]
            )
        for k in range(8):
            lanes[8 * k : 8 * k + 8, :] = columns[0][k]
        a = [
            [jnp.broadcast_to(lanes[8 * k + m : 8 * k + m + 1, :], (8, 128)) for k in range(m + 1)]
            for m in range(8)
        ]
        right = [
            jnp.broadcast_to(aug[8 * j + k : 8 * j + k + 1, :], (8, 128)) for k in range(8)
        ]
        for k in range(8):
            root = lax.rsqrt(a[k][k])
            for m in range(k + 1, 8):
                a[m][k] = a[m][k] * root
            right[k] = right[k] * root
            for column in columns[1:]:
                column[k] = column[k] * root
            for m in range(k + 1, 8):
                for n in range(k + 1, m + 1):
                    a[m][n] = a[m][n] - a[m][k] * a[n][k]
                right[m] = right[m] - a[m][k] * right[k]
                for column in columns[1:]:
                    column[m] = column[m] - column[k] * a[m][k]
        for k in range(8):
            aug[8 * j + k : 8 * j + k + 1, :] = right[k][:1]
        for i in range(j + 1, blocks):
            column = columns[i - j]
            first = column[0] * right[0] + column[1] * right[1]
            second = column[2] * right[2] + column[3] * right[3]
            third = column[4] * right[4] + column[5] * right[5]
            fourth = column[6] * right[6] + column[7] * right[7]
            rows[i] = rows[i] - ((first + second) + (third + fourth))
    out_ref[...] = aug[...].T[rank : rank + cols, :] * scale


def whitened(terms, update_t, scale):
    cols, rank = update_t.shape
    return pl.pallas_call(
        functools.partial(whitened_kernel, scale),
        out_shape=jax.ShapeDtypeStruct((cols, rank), jnp.float32),
        in_specs=[ON_CHIP, ON_CHIP],
        out_specs=ON_CHIP,
        scratch_shapes=[pltpu.VMEM((rank, 2 * rank), jnp.float32)] * 2,
        compiler_params=pltpu.CompilerParams(vmem_limit_bytes=8 * 2**20),
        name="whitened",
    )(terms, update_t)


def per_device(tensor, y_factor, x_factor):
    width_x = x_factor.shape[1]
    kept, sent, folded_part = projected(tensor, y_factor, x_factor)
    folded, come = summed_everywhere(folded_part, sent)
    parts = update_parts(kept, come, folded, lax.axis_size("z"))
    update_t, wide = own_update(exchanged(parts, "z"))
    wide = with_neighbour(with_neighbour(wide, "core"), "z")
    total_x = width_x * lax.axis_size(GX)
    return whitened(of_everyone(wide, CHIPS), update_t, float(total_x) ** 0.5).T


def solution(mesh):
    finer = Mesh(mesh.devices.reshape(2, 4, 2, 2, 8), AXES)
    in_specs = (P(None, GX, GY), P(GY, None), P(None, GX))
    out_specs = P(None, AXES)
    return jax.shard_map(
        per_device, mesh=finer, in_specs=in_specs, out_specs=out_specs, check_vma=False
    )
```

```python
import functools

import jax
import jax.numpy as jnp
from jax import lax
from jax.experimental import pallas as pl
from jax.experimental.pallas import tpu as pltpu
from jax.sharding import Mesh
from jax.sharding import PartitionSpec as P


AXES = ("y_lo", "x", "core", "y_hi", "z")
GX = ("y_lo", "x", "core")
GY = ("y_hi", "z")
CHIPS = ("y_hi", "y_lo", "x")
HIGHEST = lax.Precision.HIGHEST
EARLY = 6
ON_CHIP = pl.BlockSpec(memory_space=pltpu.VMEM)


def exchanged(tiles, axis):
    return lax.all_to_all(tiles, axis, 0, 0, tiled=True)


def of_everyone(tile, axis):
    return exchanged(jnp.broadcast_to(tile[None], (lax.axis_size(axis), *tile.shape)), axis)


def tiles_of(matrix):
    rows, cols = matrix.shape
    return matrix.reshape(rows // 8, 8, cols // 128, 128).swapaxes(1, 2).reshape(-1, 8, 128)


def from_tiles(tiles, rows, cols):
    return tiles.reshape(rows // 8, cols // 128, 8, 128).swapaxes(1, 2).reshape(rows, cols)


def from_partner(array, axis):
    return lax.ppermute(array, axis, [(i, i ^ 1) for i in range(lax.axis_size(axis))])


def with_neighbour(value, axis):
    return value + from_partner(value, axis)


def summed_everywhere(matrix, sent):
    rows, cols = matrix.shape
    tiles = tiles_of(matrix).reshape(lax.axis_size(CHIPS), -1, 128)
    own = jnp.sum(exchanged(tiles, CHIPS), axis=0)
    come = from_partner(sent, "y_hi")
    own = jnp.sum(of_everyone(own, ("core", "z")), axis=0)
    return from_tiles(of_everyone(own, CHIPS).reshape(-1, 8, 128), rows, cols), come


def rounded_parts(matrix):
    high = matrix.astype(jnp.bfloat16)
    rest = matrix - high.astype(jnp.float32)
    middle = rest.astype(jnp.bfloat16)
    low = (rest - middle.astype(jnp.float32)).astype(jnp.bfloat16)
    return high, middle, low


def project_kernel(
    tensor_ref,
    y_ref,
    x_ref,
    kept_ref,
    sent_ref,
    folded_ref,
    planes,
    y_here,
    x_here,
    arrived,
):
    depth, width_x, _ = planes.shape
    rank = y_ref.shape[0]
    half = width_x // 2
    y_copy = pltpu.make_async_copy(y_ref, y_here, arrived.at[depth])
    x_copy = pltpu.make_async_copy(x_ref, x_here, arrived.at[depth + 1])
    y_copy.start()

    def plane(z):
        return pltpu.make_async_copy(tensor_ref.at[z], planes.at[z], arrived.at[z])

    for z in range(EARLY):
        plane(z).start()
    x_copy.start()
    kept_at = pl.multiple_of(lax.axis_index("y_hi") * half, half)
    sides = ((kept_ref, kept_at), (sent_ref, pl.multiple_of(half - kept_at, half)))
    y_copy.wait()
    y_t = y_here[...]
    none = jnp.zeros_like(y_t)
    y_left, y_right = jnp.concatenate([y_t, none], axis=0), jnp.concatenate([none, y_t], axis=0)
    contract = (((1,), (1,)), ((), ()))
    pairs = depth // 2
    for step in range(pairs + 1):
        if step < pairs:
            plane(2 * step).wait()
            plane(2 * step + 1).wait()
            for z in range(2 * step + EARLY, min(2 * step + EARLY + 2, depth)):
                plane(z).start()
        if step == 1:
            x_copy.wait()
        folded = None
        for there, start in sides:
            if step < pairs:
                rows = pl.ds(start, half)
                left = lax.dot_general(
                    planes[2 * step, rows, :], y_left, contract, preferred_element_type=jnp.float32
                )
                right = lax.dot_general(
                    planes[2 * step + 1, rows, :],
                    y_right,
                    contract,
                    preferred_element_type=jnp.float32,
                )
                there[:, pl.ds(2 * rank * step, 2 * rank)] = left + right
            if step > 0:
                x_part = x_here[:, pl.ds(start, half)]
                for part in rounded_parts(there[:, pl.ds(2 * rank * (step - 1), 2 * rank)]):
                    term = jnp.dot(x_part, part, preferred_element_type=jnp.float32)
                    folded = term if folded is None else folded + term
        if step > 0:
            folded_ref[:, pl.ds(2 * rank * (step - 1), 2 * rank)] = folded


def projected(tensor, y_factor, x_factor):
    depth, width_x, width_y = tensor.shape
    rank = y_factor.shape[1]
    rows = depth * rank
    return pl.pallas_call(
        project_kernel,
        out_shape=[
            jax.ShapeDtypeStruct((n, rows), jnp.float32)
            for n in (width_x // 2, width_x // 2, rank)
        ],
        in_specs=[pl.BlockSpec(memory_space=pltpu.HBM)] * 3,
        out_specs=[ON_CHIP] * 3,
        scratch_shapes=[
            pltpu.VMEM(tensor.shape, tensor.dtype),
            pltpu.VMEM((rank, width_y), y_factor.dtype),
            pltpu.VMEM(x_factor.shape, x_factor.dtype),
            pltpu.SemaphoreType.DMA((depth + 2,)),
        ],
        compiler_params=pltpu.CompilerParams(vmem_limit_bytes=24 * 2**20),
        name="projected",
    )(*(pltpu.with_memory_space_constraint(a, pltpu.HBM) for a in (tensor, y_factor.T, x_factor)))


def update_kernel(kept_ref, come_ref, folded_ref, out_ref):
    n, rows, lanes = out_ref.shape
    rank = lanes // 2
    half = 2 * rows // n
    part = lax.dot_general(
        kept_ref[...] + come_ref[...],
        folded_ref[...],
        (((1,), (1,)), ((), ())),
        precision=HIGHEST,
        preferred_element_type=jnp.float32,
    )
    part = part.reshape(n, 2, half, rank)
    packed = jnp.concatenate([part[:, 0], part[:, 1]], axis=2)
    packed = packed.reshape(n // 2, 2, half, lanes)
    for z in range(n):
        out_ref[z] = packed[:, z % 2].reshape(rows, lanes)


def update_parts(kept, come, folded, n):
    width_x = kept.shape[0]
    rank = folded.shape[0]
    return pl.pallas_call(
        update_kernel,
        out_shape=jax.ShapeDtypeStruct((n, width_x // 4, 2 * rank), jnp.float32),
        in_specs=[ON_CHIP] * 3,
        out_specs=ON_CHIP,
        compiler_params=pltpu.CompilerParams(vmem_limit_bytes=24 * 2**20),
        name="update_parts",
    )(kept, come, folded)


def cross_kernel(parts_ref, update_ref, cross_ref, packed_ref):
    rank = update_ref.shape[1]
    half = update_ref.shape[0] // 2
    packed = jnp.sum(parts_ref[...], axis=0)
    packed_ref[...] = packed
    update_t = jnp.concatenate([packed[:, :rank], packed[:, rank:]], axis=0)
    square = lax.dot_general(
        update_t,
        update_t,
        (((0,), (0,)), ((), ())),
        precision=HIGHEST,
        preferred_element_type=jnp.float32,
    )
    cross_ref[...] = jnp.concatenate([square[: rank // 2], square[rank // 2 :]], axis=1)
    start = pl.multiple_of(lax.axis_index("z") // 2 * half, half)
    own = packed_ref[pl.ds(start, half), :]
    update_ref[...] = jnp.concatenate([own[:, :rank], own[:, rank:]], axis=0)


def own_update(parts):
    n, rows, lanes = parts.shape
    rank = lanes // 2
    return pl.pallas_call(
        cross_kernel,
        out_shape=(
            jax.ShapeDtypeStruct((4 * rows // n, rank), jnp.float32),
            jax.ShapeDtypeStruct((rank // 2, 2 * rank), jnp.float32),
        ),
        in_specs=[ON_CHIP],
        out_specs=(ON_CHIP, ON_CHIP),
        scratch_shapes=[pltpu.VMEM((rows, lanes), jnp.float32)],
        compiler_params=pltpu.CompilerParams(vmem_limit_bytes=8 * 2**20),
        name="own_update",
    )(parts)


def whitened_kernel(scale, cross_ref, update_ref, out_ref, aug, lanes):
    rank = update_ref.shape[1]
    cols = update_ref.shape[0]
    blocks = rank // 8
    wide = cross_ref[0]
    for i in range(1, cross_ref.shape[0]):
        wide = wide + cross_ref[i]
    gram = jnp.concatenate([wide[:, :rank], wide[:, rank:]], axis=0)
    padded = jnp.concatenate(
        [update_ref[...], jnp.zeros((rank - cols, rank), jnp.float32)], axis=0
    )
    aug[...] = jnp.concatenate([gram, padded.T], axis=1)
    rows = [aug[8 * i : 8 * i + 8, :] for i in range(blocks)]
    for j in range(blocks):
        aug[8 * j : 8 * j + 8, :] = rows[j]
        columns = []
        for i in range(j, blocks):
            columns.append(
                [
                    jnp.broadcast_to(rows[i][:, 8 * j + k : 8 * j + k + 1], (8, 128))
                    for k in range(8)
                ]
            )
        for k in range(8):
            lanes[8 * k : 8 * k + 8, :] = columns[0][k]
        a = [
            [jnp.broadcast_to(lanes[8 * k + m : 8 * k + m + 1, :], (8, 128)) for k in range(m + 1)]
            for m in range(8)
        ]
        right = [
            jnp.broadcast_to(aug[8 * j + k : 8 * j + k + 1, :], (8, 128)) for k in range(8)
        ]
        for k in range(8):
            root = lax.rsqrt(a[k][k])
            for m in range(k + 1, 8):
                a[m][k] = a[m][k] * root
            right[k] = right[k] * root
            for column in columns[1:]:
                column[k] = column[k] * root
            for m in range(k + 1, 8):
                for n in range(k + 1, m + 1):
                    a[m][n] = a[m][n] - a[m][k] * a[n][k]
                right[m] = right[m] - a[m][k] * right[k]
                for column in columns[1:]:
                    column[m] = column[m] - column[k] * a[m][k]
        for k in range(8):
            aug[8 * j + k : 8 * j + k + 1, :] = right[k][:1]
        for i in range(j + 1, blocks):
            column = columns[i - j]
            first = column[0] * right[0] + column[1] * right[1]
            second = column[2] * right[2] + column[3] * right[3]
            third = column[4] * right[4] + column[5] * right[5]
            fourth = column[6] * right[6] + column[7] * right[7]
            rows[i] = rows[i] - ((first + second) + (third + fourth))
    out_ref[...] = aug[...].T[rank : rank + cols, :] * scale


def whitened(terms, update_t, scale):
    cols, rank = update_t.shape
    return pl.pallas_call(
        functools.partial(whitened_kernel, scale),
        out_shape=jax.ShapeDtypeStruct((cols, rank), jnp.float32),
        in_specs=[ON_CHIP, ON_CHIP],
        out_specs=ON_CHIP,
        scratch_shapes=[pltpu.VMEM((rank, 2 * rank), jnp.float32)] * 2,
        compiler_params=pltpu.CompilerParams(vmem_limit_bytes=8 * 2**20),
        name="whitened",
    )(terms, update_t)


def new_basis(tensor, y_factor, x_factor):
    width_x = x_factor.shape[1]
    kept, sent, folded_part = projected(tensor, y_factor, x_factor)
    folded, come = summed_everywhere(folded_part, sent)
    parts = update_parts(kept, come, folded, lax.axis_size("z"))
    update_t, wide = own_update(exchanged(parts, "z"))
    wide = with_neighbour(with_neighbour(wide, "core"), "z")
    total_x = width_x * lax.axis_size(GX)
    return whitened(of_everyone(wide, CHIPS), update_t, float(total_x) ** 0.5).T


def solution(mesh):
    finer = Mesh(mesh.devices.reshape(2, 4, 2, 2, 8), AXES)
    in_specs = (P(None, GX, GY), P(GY, None), P(None, GX))
    out_specs = P(None, AXES)
    return jax.shard_map(
        new_basis, mesh=finer, in_specs=in_specs, out_specs=out_specs, check_vma=False
    )
```

```python
import functools

import jax
import jax.numpy as jnp
from jax import lax
from jax.experimental import pallas as pl
from jax.experimental.pallas import tpu as pltpu
from jax.sharding import Mesh
from jax.sharding import PartitionSpec as P


AXES = ("y_lo", "x", "core", "y_hi", "z")
GX = ("y_lo", "x", "core")
GY = ("y_hi", "z")
CHIPS = ("y_hi", "y_lo", "x")
HIGHEST = lax.Precision.HIGHEST
EARLY = 6
ON_CHIP = pl.BlockSpec(memory_space=pltpu.VMEM)


def exchanged(tiles, axis):
    return lax.all_to_all(tiles, axis, 0, 0, tiled=True)


def of_everyone(tile, axis):
    return exchanged(jnp.broadcast_to(tile[None], (lax.axis_size(axis), *tile.shape)), axis)


def tiles_of(matrix):
    rows, cols = matrix.shape
    return matrix.reshape(rows // 8, 8, cols // 128, 128).swapaxes(1, 2).reshape(-1, 8, 128)


def from_tiles(tiles, rows, cols):
    return tiles.reshape(rows // 8, cols // 128, 8, 128).swapaxes(1, 2).reshape(rows, cols)


def from_partner(array, axis):
    return lax.ppermute(array, axis, [(i, i ^ 1) for i in range(lax.axis_size(axis))])


def with_neighbour(value, axis):
    return value + from_partner(value, axis)


def summed_everywhere(matrix, sent):
    rows, cols = matrix.shape
    tiles = tiles_of(matrix).reshape(lax.axis_size(CHIPS), -1, 128)
    own = jnp.sum(exchanged(tiles, CHIPS), axis=0)
    come = from_partner(sent, "y_hi")
    own = jnp.sum(of_everyone(own, ("core", "z")), axis=0)
    return from_tiles(of_everyone(own, CHIPS).reshape(-1, 8, 128), rows, cols), come


def rounded_parts(matrix):
    high = matrix.astype(jnp.bfloat16)
    rest = matrix - high.astype(jnp.float32)
    middle = rest.astype(jnp.bfloat16)
    low = (rest - middle.astype(jnp.float32)).astype(jnp.bfloat16)
    return high, middle, low


def project_kernel(
    tensor_ref,
    y_ref,
    x_ref,
    kept_ref,
    sent_ref,
    folded_ref,
    planes,
    y_here,
    x_here,
    folded_here,
    arrived,
    left_here,
):
    depth, width_x, _ = planes.shape
    rank = y_ref.shape[0]
    half = width_x // 2
    y_copy = pltpu.make_async_copy(y_ref, y_here, arrived.at[depth])
    x_copy = pltpu.make_async_copy(x_ref, x_here, arrived.at[depth + 1])
    y_copy.start()

    def plane(z):
        return pltpu.make_async_copy(tensor_ref.at[z], planes.at[z], arrived.at[z])

    def result(pair):
        lanes = pl.ds(2 * rank * pair, 2 * rank)
        return pltpu.make_async_copy(
            folded_here.at[:, lanes], folded_ref.at[:, lanes], left_here.at[pair]
        )

    for z in range(EARLY):
        plane(z).start()
    x_copy.start()
    kept_at = pl.multiple_of(lax.axis_index("y_hi") * half, half)
    sides = ((kept_ref, kept_at), (sent_ref, pl.multiple_of(half - kept_at, half)))
    y_copy.wait()
    y_t = y_here[...]
    none = jnp.zeros_like(y_t)
    y_left, y_right = jnp.concatenate([y_t, none], axis=0), jnp.concatenate([none, y_t], axis=0)
    contract = (((1,), (1,)), ((), ()))
    pairs = depth // 2
    for step in range(pairs + 1):
        if step < pairs:
            plane(2 * step).wait()
            plane(2 * step + 1).wait()
            for z in range(2 * step + EARLY, min(2 * step + EARLY + 2, depth)):
                plane(z).start()
        if step == 1:
            x_copy.wait()
        folded = None
        for there, start in sides:
            if step < pairs:
                rows = pl.ds(start, half)
                left = lax.dot_general(
                    planes[2 * step, rows, :], y_left, contract, preferred_element_type=jnp.float32
                )
                right = lax.dot_general(
                    planes[2 * step + 1, rows, :],
                    y_right,
                    contract,
                    preferred_element_type=jnp.float32,
                )
                there[:, pl.ds(2 * rank * step, 2 * rank)] = left + right
            if step > 0:
                x_part = x_here[:, pl.ds(start, half)]
                for part in rounded_parts(there[:, pl.ds(2 * rank * (step - 1), 2 * rank)]):
                    term = jnp.dot(x_part, part, preferred_element_type=jnp.float32)
                    folded = term if folded is None else folded + term
        if step > 0:
            folded_here[:, pl.ds(2 * rank * (step - 1), 2 * rank)] = folded
            result(step - 1).start()
    for pair in range(pairs):
        result(pair).wait()


def projected(tensor, y_factor, x_factor):
    depth, width_x, width_y = tensor.shape
    rank = y_factor.shape[1]
    rows = depth * rank
    return pl.pallas_call(
        project_kernel,
        out_shape=[
            jax.ShapeDtypeStruct((n, rows), jnp.float32)
            for n in (width_x // 2, width_x // 2, rank)
        ],
        in_specs=[pl.BlockSpec(memory_space=pltpu.HBM)] * 3,
        out_specs=[ON_CHIP, ON_CHIP, pl.BlockSpec(memory_space=pltpu.HBM)],
        scratch_shapes=[
            pltpu.VMEM(tensor.shape, tensor.dtype),
            pltpu.VMEM((rank, width_y), y_factor.dtype),
            pltpu.VMEM(x_factor.shape, x_factor.dtype),
            pltpu.VMEM((rank, rows), jnp.float32),
            pltpu.SemaphoreType.DMA((depth + 2,)),
            pltpu.SemaphoreType.DMA((depth // 2,)),
        ],
        compiler_params=pltpu.CompilerParams(vmem_limit_bytes=24 * 2**20),
        name="projected",
    )(*(pltpu.with_memory_space_constraint(a, pltpu.HBM) for a in (tensor, y_factor.T, x_factor)))


def update_kernel(kept_ref, come_ref, folded_ref, out_ref):
    n, rows, lanes = out_ref.shape
    rank = lanes // 2
    half = 2 * rows // n
    part = lax.dot_general(
        kept_ref[...] + come_ref[...],
        folded_ref[...],
        (((1,), (1,)), ((), ())),
        precision=HIGHEST,
        preferred_element_type=jnp.float32,
    )
    part = part.reshape(n, 2, half, rank)
    packed = jnp.concatenate([part[:, 0], part[:, 1]], axis=2)
    packed = packed.reshape(n // 2, 2, half, lanes)
    for z in range(n):
        out_ref[z] = packed[:, z % 2].reshape(rows, lanes)


def update_parts(kept, come, folded, n):
    width_x = kept.shape[0]
    rank = folded.shape[0]
    return pl.pallas_call(
        update_kernel,
        out_shape=jax.ShapeDtypeStruct((n, width_x // 4, 2 * rank), jnp.float32),
        in_specs=[ON_CHIP] * 3,
        out_specs=ON_CHIP,
        compiler_params=pltpu.CompilerParams(vmem_limit_bytes=24 * 2**20),
        name="update_parts",
    )(kept, come, folded)


def cross_kernel(parts_ref, update_ref, cross_ref, packed_ref):
    rank = update_ref.shape[1]
    half = update_ref.shape[0] // 2
    packed = jnp.sum(parts_ref[...], axis=0)
    packed_ref[...] = packed
    update_t = jnp.concatenate([packed[:, :rank], packed[:, rank:]], axis=0)
    square = lax.dot_general(
        update_t,
        update_t,
        (((0,), (0,)), ((), ())),
        precision=HIGHEST,
        preferred_element_type=jnp.float32,
    )
    cross_ref[...] = jnp.concatenate([square[: rank // 2], square[rank // 2 :]], axis=1)
    start = pl.multiple_of(lax.axis_index("z") // 2 * half, half)
    own = packed_ref[pl.ds(start, half), :]
    update_ref[...] = jnp.concatenate([own[:, :rank], own[:, rank:]], axis=0)


def own_update(parts):
    n, rows, lanes = parts.shape
    rank = lanes // 2
    return pl.pallas_call(
        cross_kernel,
        out_shape=(
            jax.ShapeDtypeStruct((4 * rows // n, rank), jnp.float32),
            jax.ShapeDtypeStruct((rank // 2, 2 * rank), jnp.float32),
        ),
        in_specs=[ON_CHIP],
        out_specs=(ON_CHIP, ON_CHIP),
        scratch_shapes=[pltpu.VMEM((rows, lanes), jnp.float32)],
        compiler_params=pltpu.CompilerParams(vmem_limit_bytes=8 * 2**20),
        name="own_update",
    )(parts)


def whitened_kernel(scale, cross_ref, update_ref, out_ref, aug, lanes):
    rank = update_ref.shape[1]
    cols = update_ref.shape[0]
    blocks = rank // 8
    wide = cross_ref[0]
    for i in range(1, cross_ref.shape[0]):
        wide = wide + cross_ref[i]
    gram = jnp.concatenate([wide[:, :rank], wide[:, rank:]], axis=0)
    padded = jnp.concatenate(
        [update_ref[...], jnp.zeros((rank - cols, rank), jnp.float32)], axis=0
    )
    aug[...] = jnp.concatenate([gram, padded.T], axis=1)
    rows = [aug[8 * i : 8 * i + 8, :] for i in range(blocks)]
    for j in range(blocks):
        aug[8 * j : 8 * j + 8, :] = rows[j]
        columns = []
        for i in range(j, blocks):
            columns.append(
                [
                    jnp.broadcast_to(rows[i][:, 8 * j + k : 8 * j + k + 1], (8, 128))
                    for k in range(8)
                ]
            )
        for k in range(8):
            lanes[8 * k : 8 * k + 8, :] = columns[0][k]
        a = [
            [jnp.broadcast_to(lanes[8 * k + m : 8 * k + m + 1, :], (8, 128)) for k in range(m + 1)]
            for m in range(8)
        ]
        right = [
            jnp.broadcast_to(aug[8 * j + k : 8 * j + k + 1, :], (8, 128)) for k in range(8)
        ]
        for k in range(8):
            root = lax.rsqrt(a[k][k])
            for m in range(k + 1, 8):
                a[m][k] = a[m][k] * root
            right[k] = right[k] * root
            for column in columns[1:]:
                column[k] = column[k] * root
            for m in range(k + 1, 8):
                for n in range(k + 1, m + 1):
                    a[m][n] = a[m][n] - a[m][k] * a[n][k]
                right[m] = right[m] - a[m][k] * right[k]
                for column in columns[1:]:
                    column[m] = column[m] - column[k] * a[m][k]
        for k in range(8):
            aug[8 * j + k : 8 * j + k + 1, :] = right[k][:1]
        for i in range(j + 1, blocks):
            column = columns[i - j]
            first = column[0] * right[0] + column[1] * right[1]
            second = column[2] * right[2] + column[3] * right[3]
            third = column[4] * right[4] + column[5] * right[5]
            fourth = column[6] * right[6] + column[7] * right[7]
            rows[i] = rows[i] - ((first + second) + (third + fourth))
    out_ref[...] = aug[...].T[rank : rank + cols, :] * scale


def whitened(terms, update_t, scale):
    cols, rank = update_t.shape
    return pl.pallas_call(
        functools.partial(whitened_kernel, scale),
        out_shape=jax.ShapeDtypeStruct((cols, rank), jnp.float32),
        in_specs=[ON_CHIP, ON_CHIP],
        out_specs=ON_CHIP,
        scratch_shapes=[pltpu.VMEM((rank, 2 * rank), jnp.float32)] * 2,
        compiler_params=pltpu.CompilerParams(vmem_limit_bytes=8 * 2**20),
        name="whitened",
    )(terms, update_t)


def new_basis(tensor, y_factor, x_factor):
    width_x = x_factor.shape[1]
    kept, sent, folded_part = projected(tensor, y_factor, x_factor)
    folded, come = summed_everywhere(folded_part, sent)
    parts = update_parts(kept, come, folded, lax.axis_size("z"))
    update_t, wide = own_update(exchanged(parts, "z"))
    wide = with_neighbour(with_neighbour(wide, "z"), "core")
    total_x = width_x * lax.axis_size(GX)
    return whitened(of_everyone(wide, CHIPS), update_t, float(total_x) ** 0.5).T


def solution(mesh):
    finer = Mesh(mesh.devices.reshape(2, 4, 2, 2, 8), AXES)
    in_specs = (P(None, GX, GY), P(GY, None), P(None, GX))
    out_specs = P(None, AXES)
    return jax.shard_map(
        new_basis, mesh=finer, in_specs=in_specs, out_specs=out_specs, check_vma=False
    )
```
